512 devices in a mesh: section: 4 (over x), frame: 8 (over z_hi, core), patch: 16 (over z_lo, y).
Axes of the slice: x: 4, y: 8, z: 8 (z_hi: 4, z_lo: 2; z = z_hi * 2 + z_lo), core: 2. Of those that a mesh axis runs over, the one named last changes fastest.
Arguments:
- exposure: bfloat16 [8, 2, 3584, 4096], P('frame', None, ('section', 'patch')), may hold values from -6 to 6, as said below
- row_prof: bfloat16 [8, 1280, 50, 64], P('frame', ('section', 'patch')), may hold values from -0.875 to 0.875
- col_prof: bfloat16 [8, 1280, 25, 256], P('frame', ('section', 'patch')), may hold values from -1.25 to 1.25
- row_off: int32 [8, 1280], P('frame', ('section', 'patch')), may hold values from 0 to 8, as said below
- col_off: int32 [8, 1280], P('frame', ('section', 'patch')), may hold values from 0 to 3840, as said below
- dest: int32 [8, 1280], P('frame', ('section', 'patch')), may hold values from 0 to 15, as said below
- fibre_weight: float32 [8, 1280, 25], P('frame', ('section', 'patch')), may hold values from 0.2 to 5
Outputs:
- spectra_ext: float32 [8, 2048, 50, 25], P('frame', ('section', 'patch'))
- coadd: float32 [1280, 50, 25], P(('section', 'patch'))
The draws below stay inside these ranges and needn't reach their ends.
Inputs may be any that keep to these rules, and one draw needn't show every extreme that they name: `exposure`: channel 0 holds pixel values, channel 1 inverse variances between 0.25 and 4. `row_off`: offsets of patches within their band extended by 8 rows on each side. `col_off`: patches of neighbouring fibre blocks share columns. `dest`: of the 20 patches of one band (p // 20 equal) in one frame, each patch index receives 20 // 16 or (35) // 16 of them, so at most 2, and some index exactly 2.
All inputs are finite; a program needn't handle non-finite values.
Results may differ from the reference program's by a relative error of at most 0.0003.
Values may be sent and summed in bfloat16 or wider, within the bound.
A program may use at most 64 MiB of HBM per device.

```python
import math
import jax
import jax.numpy as jnp
from jax import lax

NCOL = 4096
BAND = 56
HALO = 8
FB = 20
FPB = 25
WPB = 50
PC = 256
ITERS = 6
PR = 64
OWNERS = 64
NROW = 3584
FRAMES = 8
NPATCH = 1280
CAP = 2
N_PATCH = 16


def draw_exposure(key, part):
    first_key, second_key = jax.random.split(jax.random.fold_in(key, 11))
    shape = (FRAMES, NROW, NCOL)
    values = jnp.clip(jax.random.normal(first_key, shape, jnp.float32), -6.0, 6.0)
    inverse = jnp.exp(jax.random.uniform(second_key, shape, jnp.float32, math.log(0.25), math.log(4.0)))
    return jnp.stack([values, inverse], axis=1).astype(jnp.bfloat16)


def draw_row_off(key, part):
    first_key, second_key = jax.random.split(jax.random.fold_in(key, 23))
    keys = jax.random.split(first_key, FRAMES * OWNERS)
    orders = jax.vmap(lambda one_key: jax.random.permutation(one_key, FB))(keys)
    offset = jax.random.randint(second_key, (FRAMES * OWNERS, 1), 0, HALO + 1)
    return ((orders + offset) % (HALO + 1)).reshape(FRAMES, NPATCH).astype(jnp.int32)


def draw_col_off(key, part):
    spacing = (NCOL - PC) // (FB - 1)
    starts = jnp.arange(FB, dtype=jnp.int32) * spacing
    jitter = jax.random.randint(jax.random.fold_in(key, 37), (FRAMES, OWNERS, FB), -8, 9)
    placed = jnp.clip(starts[None, None, :] + jitter, 0, NCOL - PC)
    return placed.reshape(FRAMES, NPATCH).astype(jnp.int32)


def draw_dest(key, part):
    keys = jax.random.split(jax.random.fold_in(key, 41), FRAMES * OWNERS)
    orders = jax.vmap(lambda one_key: jax.random.permutation(one_key, N_PATCH))(keys)
    wanted = jnp.arange(FB, dtype=jnp.int32) % N_PATCH
    chosen = jnp.take(orders, wanted, axis=1)
    return chosen.reshape(FRAMES, NPATCH).astype(jnp.int32)


def shard_levels(rng, dims, pieces, smallest, top_value):
    loudness = 1.0
    for dim, shards_of in pieces:
        heights = jax.random.uniform(jax.random.fold_in(jax.random.fold_in(rng, 6), dim), (shards_of,), jnp.float32, smallest / len(pieces), top_value / len(pieces))
        loudness = loudness * jnp.repeat(jnp.exp(heights), dims[dim] // shards_of).reshape((-1,) + (1,) * (len(dims) - 1 - dim))
    return loudness


def centred(own_key, dims, scale, most, pieces=(), held_as=jnp.bfloat16):
    array = scale * jax.random.normal(own_key, dims, jnp.float32)
    if pieces:
        array = array * shard_levels(own_key, dims, pieces, -0.22, 0.18)
    return jnp.clip(array, -most, most).astype(held_as)


def setup_inputs(seed: int = 0) -> dict:
    splits = jax.random.split(jax.random.key(seed), 8)
    exposure = draw_exposure(jax.random.fold_in(splits[7], 71), 0)
    row_prof = centred(splits[1], (FRAMES, NPATCH, WPB, PR), WPB ** -0.5, 0.875, ((0, 8), (1, 64)))
    col_prof = centred(splits[2], (FRAMES, NPATCH, FPB, PC), FPB ** -0.5, 1.25, ((0, 8), (1, 64)))
    row_off = draw_row_off(jax.random.fold_in(splits[7], 71), 0)
    col_off = draw_col_off(jax.random.fold_in(splits[7], 71), 0)
    dest = draw_dest(jax.random.fold_in(splits[7], 71), 0)
    fibre_weight = jnp.clip(jnp.exp(math.log(5.0) - 3.218876 * jax.random.uniform(splits[6], (FRAMES, NPATCH, FPB), jnp.float32) ** shard_levels(splits[6], (FRAMES, NPATCH, FPB), ((0, 8), (1, 64)), -0.2, 0.2)), 0.2, 5.0)
    return dict(exposure=exposure, row_prof=row_prof, col_prof=col_prof, row_off=row_off, col_off=col_off, dest=dest, fibre_weight=fibre_weight)


def extract(pixels, row_psf, col_psf):
    highest = lax.Precision.HIGHEST
    values = pixels[..., 0, :, :].astype(jnp.float32)
    inverse = pixels[..., 1, :, :].astype(jnp.float32)
    row_float = row_psf.astype(jnp.float32)
    col_float = col_psf.astype(jnp.float32)

    def normal(spectrum):
        across = jnp.einsum('...wf,...fc->...wc', spectrum, col_float, precision=highest)
        modeled = jnp.einsum('...wr,...wc->...rc', row_float, across, precision=highest)
        folded = jnp.einsum('...wr,...rc->...wc', row_float, inverse * modeled, precision=highest)
        return jnp.einsum('...wc,...fc->...wf', folded, col_float, precision=highest)

    folded = jnp.einsum('...wr,...rc->...wc', row_float, inverse * values, precision=highest)
    rhs_side = jnp.einsum('...wc,...fc->...wf', folded, col_float, precision=highest)
    estimate = jnp.zeros_like(rhs_side)
    residual = rhs_side
    direction = rhs_side
    norm_now = jnp.sum(residual * residual, axis=(-2, -1), keepdims=True)
    for sweep in range(ITERS):
        imaged = normal(direction)
        curvature = jnp.sum(direction * imaged, axis=(-2, -1), keepdims=True)
        step_size = norm_now / curvature
        estimate = estimate + step_size * direction
        residual = residual - step_size * imaged
        norm_next = jnp.sum(residual * residual, axis=(-2, -1), keepdims=True)
        direction = residual + (norm_next / norm_now) * direction
        norm_now = norm_next
    return estimate


def reference(exposure, row_prof, col_prof, row_off, col_off, dest, fibre_weight):
    bands = jnp.pad(exposure, ((0, 0), (0, 0), (HALO, HALO), (0, 0)))
    owners = (jnp.arange(NPATCH) // FB).astype(jnp.int32)
    first_rows = (owners[None, :] * BAND + row_off).astype(jnp.int32)

    def cut_patch(frame_rows, first_row, first_col):
        zero_index = jnp.zeros((), jnp.int32)
        return lax.dynamic_slice(frame_rows, (zero_index, first_row, first_col), (2, PR, PC))

    def per_frame(inputs):
        frame_rows, row_starts, col_starts, row_psf, col_psf = inputs
        blocks = jax.vmap(cut_patch, (None, 0, 0))(frame_rows, row_starts, col_starts)
        return extract(blocks, row_psf, col_psf)

    spectra = lax.map(per_frame, (bands, first_rows, col_off.astype(jnp.int32), row_prof, col_prof))
    grouped = dest.reshape(FRAMES, OWNERS, FB)
    same = grouped[:, :, :, None] == grouped[:, :, None, :]
    earlier = jnp.arange(FB)[None, :] < jnp.arange(FB)[:, None]
    slot_index = jnp.sum((same & earlier[None, None]).astype(jnp.int32), axis=-1).reshape(FRAMES, NPATCH)
    position = (((owners // N_PATCH) * N_PATCH)[None, :] + dest) * (N_PATCH * CAP)
    position = (position + ((owners % N_PATCH) * CAP)[None, :] + slot_index).astype(jnp.int32)
    frame_ids = jnp.broadcast_to(jnp.arange(FRAMES).astype(jnp.int32)[:, None], (FRAMES, NPATCH))
    spectra_ext = jnp.zeros((FRAMES, OWNERS * N_PATCH * CAP, WPB, FPB), jnp.float32)
    spectra_ext = spectra_ext.at[frame_ids, position].set(spectra)
    numerator = jnp.sum(fibre_weight[:, :, None, :] * spectra, axis=0)
    denominator = jnp.sum(fibre_weight, axis=0)
    coadd = numerator / denominator[:, None, :]
    return spectra_ext, coadd
```

```python
import functools

import jax
import jax.numpy as jnp
from jax import lax
from jax.experimental import pallas as pl
from jax.experimental.pallas import tpu as pltpu
from jax.sharding import PartitionSpec as P

HALO = 8
PC = 256
ITERS = 6
PR = 64
LANES = 128
WPB = 50
FPB = 25
MESH = pl.DeviceIdType.MESH
NT = (((1,), (1,)), ((), ()))


def halo_rows(block, width):
    axes = ("section", "patch")
    count = lax.axis_size(axes)
    forward = [(i, i + 1) for i in range(count - 1)]
    backward = [(target, source) for source, target in forward]
    rows = block.shape[2]
    low = lax.ppermute(lax.slice_in_dim(block, rows - width, None, axis=2), axes, forward)
    high = lax.ppermute(lax.slice_in_dim(block, 0, width, axis=2), axes, backward)
    return low[0], high[0]


def lane_index(shape):
    return lax.broadcasted_iota(jnp.int32, shape, len(shape) - 1)


def second_piece(value, first):
    head = value.astype(jnp.bfloat16).astype(jnp.float32)
    return jnp.where(first, value, value - head).astype(jnp.bfloat16)


def project(weighted, cols, profile, half):
    head = weighted.astype(jnp.bfloat16)
    tail = (weighted - head.astype(jnp.float32)).astype(jnp.bfloat16)
    both = jnp.concatenate([head, tail], axis=0)
    folded = lax.dot_general(cols, both, NT, preferred_element_type=jnp.float32)
    folded = folded + pltpu.roll(folded, LANES // 2, 1)
    return jnp.dot(
        second_piece(folded, half),
        jnp.concatenate([profile, profile], axis=0),
        preferred_element_type=jnp.float32,
    )


def image_of(direction, cols, profile, half, quarter):
    pieces = second_piece(direction, half)
    pieces = jnp.concatenate([pieces, pieces], axis=0)
    across = lax.dot_general(profile, pieces, NT, preferred_element_type=jnp.float32)
    return jnp.dot(
        second_piece(across, quarter),
        jnp.concatenate([cols, cols], axis=0),
        preferred_element_type=jnp.float32,
    )


def total(value):
    return jnp.sum(jnp.sum(value, axis=0, keepdims=True), axis=1, keepdims=True)


def solve_kernel(
    count, group, row_off, col_off, dest, expo, low, high, profile, cols, weight,
    send, contrib,
    ext, inverse, direction, residual, spectra, norms, source, filled,
):
    half = lane_index((32, LANES)) < LANES // 2
    quarter = lane_index((PR, PR)) < PR // 2
    lanes = lane_index((PR, LANES))
    tiles = expo.shape[2] // LANES
    for channel in range(2):
        for tile in range(tiles):
            at = slice(tile * LANES, (tile + 1) * LANES)
            ext[channel, tile, 0:HALO, :] = low[channel, :, at].astype(jnp.float32)
            ext[channel, tile, HALO:PR, :] = expo[channel, :, at].astype(jnp.float32)
            ext[channel, tile, PR:PR + HALO, :] = high[channel, :, at].astype(jnp.float32)

    for d in range(group):
        filled[d] = 0
        source[2 * d] = count
        source[2 * d + 1] = count
    for p in range(count):
        target = dest[p]
        slot = filled[target]
        source[2 * target + slot] = p
        filled[target] = slot + 1

    def cut(channel, first_tile, row, shift):
        moved = [
            pltpu.roll(ext[channel, first_tile + j, pl.ds(row, PR), :], LANES - shift, 1)
            for j in range(3)
        ]
        keep = lanes < LANES - shift
        return jnp.concatenate(
            [jnp.where(keep, moved[0], moved[1]), jnp.where(keep, moved[1], moved[2])], axis=1
        )

    for p in range(count):
        row, col = row_off[p], col_off[p]
        first_tile = col // LANES
        shift = col - first_tile * LANES
        weights = cut(1, first_tile, row, shift)
        inverse[p] = weights
        rhs = project(weights * cut(0, first_tile, row, shift), cols[p], profile[p], half)
        direction[p] = rhs
        residual[p] = rhs
        spectra[p] = jnp.zeros_like(rhs)
        norms[p] = jnp.broadcast_to(total(rhs * rhs), (8, LANES))
    spectra[count] = jnp.zeros((32, LANES), jnp.float32)

    def sweep(step, carry):
        for p in range(count):
            along = direction[p]
            modeled = image_of(along, cols[p], profile[p], half, quarter)
            imaged = project(inverse[p] * modeled, cols[p], profile[p], half)
            curvature = total(along * imaged)
            now = norms[p][0:1, 0:1]
            size = now / jnp.where(curvature > 0.0, curvature, 1.0)
            spectra[p] += size * along
            left = residual[p] - size * imaged
            residual[p] = left
            later = total(left * left)
            norms[p] = jnp.broadcast_to(later, (8, LANES))
            direction[p] = left + later / jnp.where(now > 0.0, now, 1.0) * along
        return carry

    lax.fori_loop(0, ITERS - 1, sweep, 0)
    for p in range(count):
        along = direction[p]
        modeled = image_of(along, cols[p], profile[p], half, quarter)
        curvature = 2.0 * total(jnp.sum(inverse[p] * modeled * modeled, axis=0, keepdims=True))
        spectra[p] += norms[p][0:1, 0:1] / jnp.where(curvature > 0.0, curvature, 1.0) * along

    for d in range(group):
        first = spectra[source[2 * d]]
        other = spectra[source[2 * d + 1]]
        send[d] = jnp.where(half, first, other)[0:FPB]

    pairs = count // 2
    per_half = pairs // 2
    marked = lane_index((32, LANES)) % (LANES // 2) == WPB
    for j in range(pairs):
        first = jnp.broadcast_to(weight[:, j:j + 1], (32, LANES))
        other = jnp.broadcast_to(weight[:, pairs + j:pairs + j + 1], (32, LANES))
        scale = jnp.where(half, first, other)
        value = scale * jnp.where(marked, 1.0, jnp.where(half, spectra[j], spectra[pairs + j]))
        start = (j % per_half) * FPB
        contrib[j // per_half, start:start + FPB, :] = value[0:FPB]
    for h in range(2):
        contrib[h, per_half * FPB:, :] = jnp.zeros((LANES - per_half * FPB, LANES), jnp.float32)


def exchange_kernel(group, frames, send, contrib, recv, sums, arrived, gathered, out_sem, in_sem,
                    pair_sem, peer_out, peer_in, back_sem):
    me = lax.axis_index("patch")
    frame = lax.axis_index("frame")
    core = lax.rem(frame, 2)
    chip = frame // 2
    chips = frames // 2
    partner = frame + 1 - 2 * core
    barrier = pltpu.get_barrier_semaphore()
    for k in range(1, group):
        pl.semaphore_signal(barrier, inc=1, device_id={"patch": lax.rem(me + k, group)}, device_id_type=MESH)
    pl.semaphore_signal(barrier, inc=1, device_id={"frame": partner}, device_id_type=MESH)
    for k in range(1, chips):
        pl.semaphore_signal(barrier, inc=1, device_id={"frame": lax.rem(frame + 2 * k, frames)}, device_id_type=MESH)
    pl.semaphore_wait(barrier, group + chips - 1)

    swap = pltpu.make_async_remote_copy(
        contrib.at[1 - core], arrived, pair_sem.at[0], pair_sem.at[1],
        device_id={"frame": partner}, device_id_type=MESH)
    swap.start()
    copies = []
    for k in range(1, group):
        to = lax.rem(me + k, group)
        copies.append(pltpu.make_async_remote_copy(
            send.at[to], recv.at[me], out_sem.at[k], in_sem.at[k],
            device_id={"patch": to}, device_id_type=MESH))
        copies[-1].start()
    recv[me] = send[me]
    swap.wait()
    gathered[chip] = contrib[core] + arrived[...]
    peers = []
    for k in range(1, chips):
        peers.append(pltpu.make_async_remote_copy(
            gathered.at[chip], gathered.at[chip], peer_out.at[k], peer_in.at[k],
            device_id={"frame": lax.rem(frame + 2 * k, frames)}, device_id_type=MESH))
        peers[-1].start()
    for copy in peers:
        copy.wait()
    whole = gathered[0]
    for k in range(1, chips):
        whole = whole + gathered[k]
    sums[core] = whole
    back = pltpu.make_async_remote_copy(
        sums.at[core], sums.at[core], back_sem.at[0], back_sem.at[1],
        device_id={"frame": partner}, device_id_type=MESH)
    back.start()
    for copy in copies:
        copy.wait()
    back.wait()


def format_kernel(count, group, recv, sums, ext_out, coadd_out):
    pairs = count // 2
    per_half = pairs // 2
    for k in range(FPB):
        rows = recv[:, k, :]
        ext_out[k, pl.ds(0, group, stride=2), :] = rows[:, 0:WPB]
        ext_out[k, pl.ds(1, group, stride=2), :] = pltpu.roll(rows, LANES // 2, 1)[:, 0:WPB]
        for h in range(2):
            rows = sums[h, pl.ds(k, per_half, stride=FPB), :]
            for s in range(2):
                here = rows if s == 0 else pltpu.roll(rows, LANES // 2, 1)
                start = s * pairs + h * per_half
                coadd_out[k, start:start + per_half, :] = here[:, 0:WPB] / here[:, WPB:WPB + 1]


VMEM = pl.BlockSpec(memory_space=pltpu.VMEM)
SMEM = pl.BlockSpec(memory_space=pltpu.SMEM)


def local(exposure, row_prof, col_prof, row_off, col_off, dest, fibre_weight):
    group = lax.axis_size("patch")
    frames = lax.axis_size("frame")
    count = dest.shape[1]
    f32 = jnp.float32
    low, high = halo_rows(exposure, HALO)
    profile = jnp.swapaxes(row_prof[0], 1, 2)
    profile = jnp.pad(profile, ((0, 0), (0, 0), (0, LANES // 2 - WPB)))
    profile = jnp.concatenate([profile, profile], axis=2)
    cols = jnp.pad(col_prof[0], ((0, 0), (0, 32 - FPB), (0, 0)))
    weight = jnp.pad(fibre_weight[0].T, ((0, 32 - FPB), (0, LANES - count)))
    tiles = exposure.shape[3] // LANES
    send, contrib = pl.pallas_call(
        functools.partial(solve_kernel, count, group),
        out_shape=(
            jax.ShapeDtypeStruct((group, FPB, LANES), f32),
            jax.ShapeDtypeStruct((2, LANES, LANES), f32),
        ),
        in_specs=[SMEM] * 3 + [VMEM] * 6,
        out_specs=(VMEM, VMEM),
        scratch_shapes=[
            pltpu.VMEM((2, tiles + 1, PR + HALO, LANES), f32),
            pltpu.VMEM((count, PR, PC), f32),
            pltpu.VMEM((count, 32, LANES), f32),
            pltpu.VMEM((count, 32, LANES), f32),
            pltpu.VMEM((count + 1, 32, LANES), f32),
            pltpu.VMEM((count, 8, LANES), f32),
            pltpu.SMEM((2 * group,), jnp.int32),
            pltpu.SMEM((group,), jnp.int32),
        ],
        compiler_params=pltpu.CompilerParams(vmem_limit_bytes=40 << 20),
        name="solve",
    )(row_off[0], col_off[0], dest[0], exposure[0], low, high, profile, cols, weight)
    chips = frames // 2
    recv, sums = pl.pallas_call(
        functools.partial(exchange_kernel, group, frames),
        out_shape=(
            jax.ShapeDtypeStruct((group, FPB, LANES), f32),
            jax.ShapeDtypeStruct((2, LANES, LANES), f32),
        ),
        in_specs=[VMEM] * 2,
        out_specs=(VMEM, VMEM),
        scratch_shapes=[
            pltpu.VMEM((LANES, LANES), f32),
            pltpu.VMEM((chips, LANES, LANES), f32),
            pltpu.SemaphoreType.DMA((group,)),
            pltpu.SemaphoreType.DMA((group,)),
            pltpu.SemaphoreType.DMA((2,)),
            pltpu.SemaphoreType.DMA((chips,)),
            pltpu.SemaphoreType.DMA((chips,)),
            pltpu.SemaphoreType.DMA((2,)),
        ],
        compiler_params=pltpu.CompilerParams(collective_id=0, has_side_effects=True),
        name="exchange",
    )(send, contrib)
    ext_out, coadd_out = pl.pallas_call(
        functools.partial(format_kernel, count, group),
        out_shape=(
            jax.ShapeDtypeStruct((FPB, 2 * group, WPB), f32),
            jax.ShapeDtypeStruct((FPB, count, WPB), f32),
        ),
        in_specs=[VMEM] * 2,
        out_specs=(VMEM, VMEM),
        name="arrange",
    )(recv, sums)
    return jnp.transpose(ext_out, (1, 2, 0))[None], jnp.transpose(coadd_out, (1, 2, 0))


def solution(mesh):
    in_specs = (
        P("frame", None, ("section", "patch"), None),
        P("frame", ("section", "patch"), None, None),
        P("frame", ("section", "patch"), None, None),
        P("frame", ("section", "patch")),
        P("frame", ("section", "patch")),
        P("frame", ("section", "patch")),
        P("frame", ("section", "patch"), None),
    )
    out_specs = (P("frame", ("section", "patch"), None, None), P(("section", "patch"), None, None))
    return jax.shard_map(local, mesh=mesh, in_specs=in_specs, out_specs=out_specs, check_vma=False)
```

```python
import functools

import jax
import jax.numpy as jnp
from jax import lax
from jax.experimental import pallas as pl
from jax.experimental.pallas import tpu as pltpu
from jax.sharding import PartitionSpec as P

HALO = 8
PC = 256
ITERS = 6
PR = 64
LANES = 128
WPB = 50
FPB = 25
BATCH = 20
MESH = pl.DeviceIdType.MESH
NT = (((1,), (1,)), ((), ()))


def halo_rows(block, width):
    axes = ("section", "patch")
    count = lax.axis_size(axes)
    forward = [(i, i + 1) for i in range(count - 1)]
    backward = [(target, source) for source, target in forward]
    rows = block.shape[2]
    low = lax.ppermute(lax.slice_in_dim(block, rows - width, None, axis=2), axes, forward)
    high = lax.ppermute(lax.slice_in_dim(block, 0, width, axis=2), axes, backward)
    return low[0], high[0]


def lane_index(shape):
    return lax.broadcasted_iota(jnp.int32, shape, len(shape) - 1)


def second_piece(value, first):
    head = value.astype(jnp.bfloat16).astype(jnp.float32)
    return jnp.where(first, value, value - head).astype(jnp.bfloat16)


def project(weighted, cols, profile, half):
    head = [g.astype(jnp.bfloat16) for g in weighted]
    tail = [(g - h.astype(jnp.float32)).astype(jnp.bfloat16) for g, h in zip(weighted, head)]
    both = [jnp.concatenate([h, t], axis=0) for h, t in zip(head, tail)]
    folded = [
        lax.dot_general(c, g, NT, preferred_element_type=jnp.float32) for c, g in zip(cols, both)
    ]
    folded = [f + pltpu.roll(f, LANES // 2, 1) for f in folded]
    pieces = [second_piece(f, half) for f in folded]
    return [
        jnp.dot(f, jnp.concatenate([r, r], axis=0), preferred_element_type=jnp.float32)
        for f, r in zip(pieces, profile)
    ]


def image_of(direction, cols, profile, half, quarter):
    pieces = [second_piece(d, half) for d in direction]
    pieces = [jnp.concatenate([d, d], axis=0) for d in pieces]
    across = [
        lax.dot_general(r, d, NT, preferred_element_type=jnp.float32) for r, d in zip(profile, pieces)
    ]
    pieces = [second_piece(u, quarter) for u in across]
    return [
        jnp.dot(u, jnp.concatenate([c, c], axis=0), preferred_element_type=jnp.float32)
        for u, c in zip(pieces, cols)
    ]


def total(value):
    return jnp.sum(jnp.sum(value, axis=0, keepdims=True), axis=1, keepdims=True)


def solve_kernel(
    count, group, row_off, col_off, dest, expo, low, high, profile, cols, weight,
    send, contrib,
    ext, inverse, direction, residual, spectra, norms, source, filled,
):
    half = lane_index((32, LANES)) < LANES // 2
    quarter = lane_index((PR, PR)) < PR // 2
    lanes = lane_index((PR, LANES))
    tiles = expo.shape[2] // LANES
    for channel in range(2):
        for tile in range(tiles):
            at = slice(tile * LANES, (tile + 1) * LANES)
            ext[channel, tile, 0:HALO, :] = low[channel, :, at].astype(jnp.float32)
            ext[channel, tile, HALO:PR, :] = expo[channel, :, at].astype(jnp.float32)
            ext[channel, tile, PR:PR + HALO, :] = high[channel, :, at].astype(jnp.float32)

    for d in range(group):
        filled[d] = 0
        source[2 * d] = count
        source[2 * d + 1] = count
    for p in range(count):
        target = dest[p]
        slot = filled[target]
        source[2 * target + slot] = p
        filled[target] = slot + 1

    def cut(channel, first_tile, row, shift):
        moved = [
            pltpu.roll(ext[channel, first_tile + j, pl.ds(row, PR), :], LANES - shift, 1)
            for j in range(3)
        ]
        keep = lanes < LANES - shift
        return jnp.concatenate(
            [jnp.where(keep, moved[0], moved[1]), jnp.where(keep, moved[1], moved[2])], axis=1
        )

    def start(ps):
        weighted = []
        for p in ps:
            row, col = row_off[p], col_off[p]
            first_tile = col // LANES
            shift = col - first_tile * LANES
            weights = cut(1, first_tile, row, shift)
            inverse[p] = weights
            weighted.append(weights * cut(0, first_tile, row, shift))
        rhs = project(weighted, [cols[p] for p in ps], [profile[p] for p in ps], half)
        for p, value in zip(ps, rhs):
            direction[p] = value
            residual[p] = value
            spectra[p] = jnp.zeros_like(value)
            norms[p] = jnp.broadcast_to(total(value * value), (8, LANES))

    def sweep(ps):
        c = [cols[p] for p in ps]
        r = [profile[p] for p in ps]
        along = [direction[p] for p in ps]
        modeled = image_of(along, c, r, half, quarter)
        imaged = project([inverse[p] * m for p, m in zip(ps, modeled)], c, r, half)
        curvature = [total(d * q) for d, q in zip(along, imaged)]
        now = [norms[p][0:1, 0:1] for p in ps]
        size = [n / jnp.where(k > 0.0, k, 1.0) for n, k in zip(now, curvature)]
        left = [residual[p] - a * q for p, a, q in zip(ps, size, imaged)]
        later = [total(e * e) for e in left]
        ratio = [n / jnp.where(b > 0.0, b, 1.0) for n, b in zip(later, now)]
        for p, a, d, e, n, k in zip(ps, size, along, left, later, ratio):
            spectra[p] += a * d
            residual[p] = e
            norms[p] = jnp.broadcast_to(n, (8, LANES))
            direction[p] = e + k * d

    def finish(ps):
        c = [cols[p] for p in ps]
        r = [profile[p] for p in ps]
        along = [direction[p] for p in ps]
        modeled = image_of(along, c, r, half, quarter)
        curvature = [
            2.0 * total(jnp.sum(inverse[p] * m * m, axis=0, keepdims=True)) for p, m in zip(ps, modeled)
        ]
        for p, d, k in zip(ps, along, curvature):
            spectra[p] += norms[p][0:1, 0:1] / jnp.where(k > 0.0, k, 1.0) * d

    sets = [list(range(first, first + BATCH)) for first in range(0, count, BATCH)]
    for ps in sets:
        start(ps)
    spectra[count] = jnp.zeros((32, LANES), jnp.float32)

    def step(index, carry):
        for ps in sets:
            sweep(ps)
        return carry

    lax.fori_loop(0, ITERS - 1, step, 0)
    for ps in sets:
        finish(ps)

    for d in range(group):
        first = spectra[source[2 * d]]
        other = spectra[source[2 * d + 1]]
        send[d] = jnp.where(half, first, other)[0:FPB]

    pairs = count // 2
    per_half = pairs // 2
    marked = lane_index((32, LANES)) % (LANES // 2) == WPB
    for j in range(pairs):
        first = jnp.broadcast_to(weight[:, j:j + 1], (32, LANES))
        other = jnp.broadcast_to(weight[:, pairs + j:pairs + j + 1], (32, LANES))
        scale = jnp.where(half, first, other)
        value = scale * jnp.where(marked, 1.0, jnp.where(half, spectra[j], spectra[pairs + j]))
        start = (j % per_half) * FPB
        contrib[j // per_half, start:start + FPB, :] = value[0:FPB]
    for h in range(2):
        contrib[h, per_half * FPB:, :] = jnp.zeros((LANES - per_half * FPB, LANES), jnp.float32)


def exchange_kernel(group, frames, send, contrib, recv, sums, arrived, gathered, out_sem, in_sem,
                    pair_sem, peer_out, peer_in, back_sem):
    me = lax.axis_index("patch")
    frame = lax.axis_index("frame")
    core = lax.rem(frame, 2)
    chip = frame // 2
    chips = frames // 2
    partner = frame + 1 - 2 * core
    barrier = pltpu.get_barrier_semaphore()
    for k in range(1, group):
        pl.semaphore_signal(barrier, inc=1, device_id={"patch": lax.rem(me + k, group)}, device_id_type=MESH)
    pl.semaphore_signal(barrier, inc=1, device_id={"frame": partner}, device_id_type=MESH)
    for k in range(1, chips):
        pl.semaphore_signal(barrier, inc=1, device_id={"frame": lax.rem(frame + 2 * k, frames)}, device_id_type=MESH)
    pl.semaphore_wait(barrier, group + chips - 1)

    swap = pltpu.make_async_remote_copy(
        contrib.at[1 - core], arrived, pair_sem.at[0], pair_sem.at[1],
        device_id={"frame": partner}, device_id_type=MESH)
    swap.start()
    copies = []
    for k in range(1, group):
        to = lax.rem(me + k, group)
        copies.append(pltpu.make_async_remote_copy(
            send.at[to], recv.at[me], out_sem.at[k], in_sem.at[k],
            device_id={"patch": to}, device_id_type=MESH))
        copies[-1].start()
    recv[me] = send[me]
    swap.wait()
    gathered[chip] = contrib[core] + arrived[...]
    peers = []
    for k in range(1, chips):
        peers.append(pltpu.make_async_remote_copy(
            gathered.at[chip], gathered.at[chip], peer_out.at[k], peer_in.at[k],
            device_id={"frame": lax.rem(frame + 2 * k, frames)}, device_id_type=MESH))
        peers[-1].start()
    for copy in peers:
        copy.wait()
    whole = gathered[0]
    for k in range(1, chips):
        whole = whole + gathered[k]
    sums[core] = whole
    back = pltpu.make_async_remote_copy(
        sums.at[core], sums.at[core], back_sem.at[0], back_sem.at[1],
        device_id={"frame": partner}, device_id_type=MESH)
    back.start()
    for copy in copies:
        copy.wait()
    back.wait()


def format_kernel(count, group, recv, sums, ext_out, coadd_out):
    pairs = count // 2
    per_half = pairs // 2
    for k in range(FPB):
        rows = recv[:, k, :]
        ext_out[k, pl.ds(0, group, stride=2), :] = rows[:, 0:WPB]
        ext_out[k, pl.ds(1, group, stride=2), :] = pltpu.roll(rows, LANES // 2, 1)[:, 0:WPB]
        for h in range(2):
            rows = sums[h, pl.ds(k, per_half, stride=FPB), :]
            for s in range(2):
                here = rows if s == 0 else pltpu.roll(rows, LANES // 2, 1)
                start = s * pairs + h * per_half
                coadd_out[k, start:start + per_half, :] = here[:, 0:WPB] / here[:, WPB:WPB + 1]


VMEM = pl.BlockSpec(memory_space=pltpu.VMEM)
SMEM = pl.BlockSpec(memory_space=pltpu.SMEM)


def solve_call(count, group, row_off, col_off, dest, exposure, low, high, row_prof, col_prof, fibre_weight):
    f32 = jnp.float32
    profile = jnp.swapaxes(row_prof, 1, 2)
    profile = jnp.pad(profile, ((0, 0), (0, 0), (0, LANES // 2 - WPB)))
    profile = jnp.concatenate([profile, profile], axis=2)
    cols = jnp.pad(col_prof, ((0, 0), (0, 32 - FPB), (0, 0)))
    weight = jnp.pad(fibre_weight.T, ((0, 32 - FPB), (0, LANES - count)))
    tiles = exposure.shape[2] // LANES
    return pl.pallas_call(
        functools.partial(solve_kernel, count, group),
        out_shape=(
            jax.ShapeDtypeStruct((group, FPB, LANES), f32),
            jax.ShapeDtypeStruct((2, LANES, LANES), f32),
        ),
        in_specs=[SMEM] * 3 + [VMEM] * 6,
        out_specs=(VMEM, VMEM),
        scratch_shapes=[
            pltpu.VMEM((2, tiles + 1, PR + HALO, LANES), f32),
            pltpu.VMEM((count, PR, PC), f32),
            pltpu.VMEM((count, 32, LANES), f32),
            pltpu.VMEM((count, 32, LANES), f32),
            pltpu.VMEM((count + 1, 32, LANES), f32),
            pltpu.VMEM((count, 8, LANES), f32),
            pltpu.SMEM((2 * group,), jnp.int32),
            pltpu.SMEM((group,), jnp.int32),
        ],
        compiler_params=pltpu.CompilerParams(vmem_limit_bytes=40 << 20),
        name="solve",
    )(row_off, col_off, dest, exposure, low, high, profile, cols, weight)


def local(exposure, row_prof, col_prof, row_off, col_off, dest, fibre_weight):
    group = lax.axis_size("patch")
    frames = lax.axis_size("frame")
    count = dest.shape[1]
    f32 = jnp.float32
    low, high = halo_rows(exposure, HALO)
    send, contrib = solve_call(
        count, group, row_off[0], col_off[0], dest[0], exposure[0], low, high,
        row_prof[0], col_prof[0], fibre_weight[0])
    chips = frames // 2
    recv, sums = pl.pallas_call(
        functools.partial(exchange_kernel, group, frames),
        out_shape=(
            jax.ShapeDtypeStruct((group, FPB, LANES), f32),
            jax.ShapeDtypeStruct((2, LANES, LANES), f32),
        ),
        in_specs=[VMEM] * 2,
        out_specs=(VMEM, VMEM),
        scratch_shapes=[
            pltpu.VMEM((LANES, LANES), f32),
            pltpu.VMEM((chips, LANES, LANES), f32),
            pltpu.SemaphoreType.DMA((group,)),
            pltpu.SemaphoreType.DMA((group,)),
            pltpu.SemaphoreType.DMA((2,)),
            pltpu.SemaphoreType.DMA((chips,)),
            pltpu.SemaphoreType.DMA((chips,)),
            pltpu.SemaphoreType.DMA((2,)),
        ],
        compiler_params=pltpu.CompilerParams(collective_id=0, has_side_effects=True),
        name="exchange",
    )(send, contrib)
    ext_out, coadd_out = pl.pallas_call(
        functools.partial(format_kernel, count, group),
        out_shape=(
            jax.ShapeDtypeStruct((FPB, 2 * group, WPB), f32),
            jax.ShapeDtypeStruct((FPB, count, WPB), f32),
        ),
        in_specs=[VMEM] * 2,
        out_specs=(VMEM, VMEM),
        name="arrange",
    )(recv, sums)
    return jnp.transpose(ext_out, (1, 2, 0))[None], jnp.transpose(coadd_out, (1, 2, 0))


def solution(mesh):
    in_specs = (
        P("frame", None, ("section", "patch"), None),
        P("frame", ("section", "patch"), None, None),
        P("frame", ("section", "patch"), None, None),
        P("frame", ("section", "patch")),
        P("frame", ("section", "patch")),
        P("frame", ("section", "patch")),
        P("frame", ("section", "patch"), None),
    )
    out_specs = (P("frame", ("section", "patch"), None, None), P(("section", "patch"), None, None))
    return jax.shard_map(local, mesh=mesh, in_specs=in_specs, out_specs=out_specs, check_vma=False)
```

```python
import functools

import jax
import jax.numpy as jnp
from jax import lax
from jax.experimental import pallas as pl
from jax.experimental.pallas import tpu as pltpu
from jax.sharding import PartitionSpec as P

HALO = 8
PC = 256
ITERS = 6
PR = 64
LANES = 128
WPB = 50
FPB = 25
MESH = pl.DeviceIdType.MESH
NT = (((1,), (1,)), ((), ()))


def lane_index(shape):
    return lax.broadcasted_iota(jnp.int32, shape, len(shape) - 1)


def second_piece(value, first):
    head = value.astype(jnp.bfloat16).astype(jnp.float32)
    return jnp.where(first, value, value - head).astype(jnp.bfloat16)


def project(weighted, cols, profile, half):
    head = [g.astype(jnp.bfloat16) for g in weighted]
    tail = [(g - h.astype(jnp.float32)).astype(jnp.bfloat16) for g, h in zip(weighted, head)]
    both = [jnp.concatenate([h, t], axis=0) for h, t in zip(head, tail)]
    folded = [
        lax.dot_general(c, g, NT, preferred_element_type=jnp.float32) for c, g in zip(cols, both)
    ]
    folded = [f + pltpu.roll(f, LANES // 2, 1) for f in folded]
    pieces = [second_piece(f, half) for f in folded]
    return [
        jnp.dot(f, jnp.concatenate([r, r], axis=0), preferred_element_type=jnp.float32)
        for f, r in zip(pieces, profile)
    ]


def image_of(direction, cols, profile, half, quarter):
    pieces = [second_piece(d, half) for d in direction]
    pieces = [jnp.concatenate([d, d], axis=0) for d in pieces]
    across = [
        lax.dot_general(r, d, NT, preferred_element_type=jnp.float32) for r, d in zip(profile, pieces)
    ]
    pieces = [second_piece(u, quarter) for u in across]
    return [
        jnp.dot(u, jnp.concatenate([c, c], axis=0), preferred_element_type=jnp.float32)
        for u, c in zip(pieces, cols)
    ]


def total(value):
    return jnp.sum(jnp.sum(value, axis=0, keepdims=True), axis=1, keepdims=True)


def solve_kernel(
    count, group, frames,
    row_off, col_off, dest, exposure, row_prof, col_prof, fibre_weight,
    ext_out, coadd_out,
    pixels, rows_raw, cols_raw, weight_raw, low, high, ext, cols_wide, profile, cols,
    cut_weight, cut_value, inverse, direction, residual, spectra, norms, send, recv, contrib,
    arrived, mine, parts, sums,
    load_sem, halo_out, halo_in, swap_sem, out_sem, in_sem, part_out, part_in, sum_out, sum_in, fwd_out, fwd_in,
):
    f32 = jnp.float32
    section = lax.axis_index("section")
    frame = lax.axis_index("frame")
    me = lax.axis_index("patch")
    sections = lax.axis_size("section")
    core = lax.rem(frame, 2)
    chip = frame // 2
    chips = frames // 2
    partner = frame + 1 - 2 * core
    band = section * group + me
    bands = sections * group
    above = lax.rem(band + bands - 1, bands)
    below = lax.rem(band + 1, bands)

    def at_band(index):
        return {"section": index // group, "patch": lax.rem(index, group)}

    barrier = pltpu.get_barrier_semaphore()
    inner = [{"patch": lax.rem(me + k, group)} for k in range(1, group)]
    peers = [{"frame": lax.rem(frame + 2 * k, frames)} for k in range(1, chips)]
    partners = [at_band(above), at_band(below)] + [{"frame": partner}] + peers + inner
    for device in partners:
        pl.semaphore_signal(barrier, inc=1, device_id=device, device_id_type=MESH)
    loads = [
        pltpu.make_async_copy(source, target, load_sem.at[i])
        for i, (source, target) in enumerate(
            [(exposure, pixels), (row_prof, rows_raw), (col_prof, cols_raw), (fibre_weight, weight_raw)]
        )
    ]
    for load in loads:
        load.start()
    pl.semaphore_wait(barrier, len(partners))

    depth = exposure.shape[1]
    down = pltpu.make_async_remote_copy(
        exposure.at[:, depth - HALO:depth, :], low, halo_out.at[0], halo_in.at[0],
        device_id=at_band(below), device_id_type=MESH)
    up = pltpu.make_async_remote_copy(
        exposure.at[:, 0:HALO, :], high, halo_out.at[1], halo_in.at[1],
        device_id=at_band(above), device_id_type=MESH)
    down.start()
    up.start()

    half = lane_index((32, LANES)) < LANES // 2
    quarter = lane_index((PR, PR)) < PR // 2
    tiles = exposure.shape[2] // LANES

    loads[1].wait()
    for p in range(count):
        turned = jnp.pad(rows_raw[p].astype(f32), ((0, PR - WPB), (0, LANES - PR))).T[0:PR]
        profile[p] = jnp.concatenate([turned, turned], axis=1).astype(jnp.bfloat16)
    loads[2].wait()
    stride = cols_wide.shape[1] // FPB
    for k in range(FPB):
        for j in range(2):
            cols_wide[j, k * stride:k * stride + count, :] = (
                cols_raw[k, :, j * LANES:(j + 1) * LANES].astype(f32))
    gap = jnp.zeros((32 - FPB, PC), f32)
    for p in range(count):
        taken = [cols_wide[j, pl.ds(p, FPB, stride=stride), :] for j in range(2)]
        cols[p] = jnp.concatenate([jnp.concatenate(taken, axis=1), gap], axis=0).astype(jnp.bfloat16)

    loads[0].wait()
    for channel in range(2):
        for tile in range(tiles):
            at = slice(tile * LANES, (tile + 1) * LANES)
            ext[channel, tile, HALO:PR, :] = pixels[channel, :, at].astype(f32)

    starts = [row_off[p] for p in range(count)]
    columns = [col_off[p] for p in range(count)]
    firsts = [c // LANES for c in columns]
    shifts = [c - t * LANES for c, t in zip(columns, firsts)]

    def cut(first, size):
        lanes = lane_index((size, LANES))
        for p in range(count):
            keep = lanes < LANES - shifts[p]
            moved = [
                [
                    pltpu.roll(ext[channel, firsts[p] + j, first:first + size, :], LANES - shifts[p], 1)
                    for j in range(3)
                ]
                for channel in range(2)
            ]
            for j in range(2):
                value, weight = [jnp.where(keep, m[j], m[j + 1]) for m in moved]
                cut_weight[p, j, first:first + size, :] = weight
                cut_value[p, j, first:first + size, :] = weight * value

    cut(HALO, PR - HALO)
    loads[3].wait()
    raw = jnp.concatenate([weight_raw[...], jnp.zeros((count, LANES - FPB), f32)], axis=1)
    weights = jnp.concatenate([raw, jnp.zeros((LANES - count, LANES), f32)], axis=0).T[0:32]

    source = []
    for d in range(group):
        first = jnp.int32(count)
        last = jnp.int32(count)
        for p in range(count):
            last = jnp.where(dest[p] == d, p, last)
            first = jnp.where(dest[count - 1 - p] == d, count - 1 - p, first)
        source.append((first, jnp.where(last == first, count, last)))

    down.wait_recv()
    up.wait_recv()
    for channel in range(2):
        for tile in range(tiles):
            at = slice(tile * LANES, (tile + 1) * LANES)
            ext[channel, tile, 0:HALO, :] = jnp.where(band > 0, low[channel, :, at].astype(f32), 0.0)
            ext[channel, tile, PR:PR + HALO, :] = jnp.where(
                band < bands - 1, high[channel, :, at].astype(f32), 0.0)
    cut(0, HALO)
    cut(PR, HALO)

    every = list(range(count))
    c = [cols[p] for p in every]
    r = [profile[p] for p in every]
    weighted = []
    for p in every:
        inverse[p] = jnp.concatenate([cut_weight[p, j, pl.ds(starts[p], PR), :] for j in range(2)], axis=1)
        weighted.append(
            jnp.concatenate([cut_value[p, j, pl.ds(starts[p], PR), :] for j in range(2)], axis=1))
    for p, value in zip(every, project(weighted, c, r, half)):
        direction[p] = value
        residual[p] = value
        spectra[p] = jnp.zeros_like(value)
        norms[p] = jnp.broadcast_to(total(value * value), (8, LANES))
    spectra[count] = jnp.zeros((32, LANES), f32)

    def sweep(index, carry):
        c = [cols[p] for p in every]
        r = [profile[p] for p in every]
        along = [direction[p] for p in every]
        modeled = image_of(along, c, r, half, quarter)
        imaged = project([inverse[p] * m for p, m in zip(every, modeled)], c, r, half)
        curvature = [total(d * q) for d, q in zip(along, imaged)]
        now = [norms[p][0:1, 0:1] for p in every]
        size = [n / jnp.where(k > 0.0, k, 1.0) for n, k in zip(now, curvature)]
        left = [residual[p] - a * q for p, a, q in zip(every, size, imaged)]
        later = [total(e * e) for e in left]
        ratio = [n / jnp.where(b > 0.0, b, 1.0) for n, b in zip(later, now)]
        for p, a, d, e, n, k in zip(every, size, along, left, later, ratio):
            spectra[p] += a * d
            residual[p] = e
            norms[p] = jnp.broadcast_to(n, (8, LANES))
            direction[p] = e + k * d
        return carry

    lax.fori_loop(0, ITERS - 1, sweep, 0)
    along = [direction[p] for p in every]
    modeled = image_of(along, [cols[p] for p in every], [profile[p] for p in every], half, quarter)
    curvature = [
        2.0 * total(jnp.sum(inverse[p] * m * m, axis=0, keepdims=True)) for p, m in zip(every, modeled)
    ]
    for p, d, k in zip(every, along, curvature):
        spectra[p] += norms[p][0:1, 0:1] / jnp.where(k > 0.0, k, 1.0) * d

    pairs = count // 2
    per_half = pairs // 2
    marked = lane_index((32, LANES)) % (LANES // 2) == WPB
    for j in range(pairs):
        scale = jnp.where(
            half,
            jnp.broadcast_to(weights[:, j:j + 1], (32, LANES)),
            jnp.broadcast_to(weights[:, pairs + j:pairs + j + 1], (32, LANES)))
        value = scale * jnp.where(marked, 1.0, jnp.where(half, spectra[j], spectra[pairs + j]))
        start = (j % per_half) * FPB
        contrib[j // per_half, start:start + FPB, :] = value[0:FPB]
    for h in range(2):
        contrib[h, per_half * FPB:, :] = jnp.zeros((LANES - per_half * FPB, LANES), f32)
    swap = pltpu.make_async_remote_copy(
        contrib.at[1 - core], arrived, swap_sem.at[0], swap_sem.at[1],
        device_id={"frame": partner}, device_id_type=MESH)
    swap.start()
    for d in range(group):
        send[d] = jnp.where(half, spectra[source[d][0]], spectra[source[d][1]])[0:FPB]
    spread = []
    for k in range(1, group):
        to = lax.rem(me + k, group)
        spread.append(pltpu.make_async_remote_copy(
            send.at[to], recv.at[me], out_sem.at[k], in_sem.at[k],
            device_id={"patch": to}, device_id_type=MESH))
        spread[-1].start()

    def chunk(index):
        return pl.ds(pl.multiple_of(index * 32, 32), 32)

    swap.wait()
    mine[...] = contrib[core] + arrived[...]
    scatter = []
    for k in range(1, chips):
        to = lax.rem(chip + k, chips)
        scatter.append(pltpu.make_async_remote_copy(
            mine.at[chunk(to)], parts.at[chip], part_out.at[k], part_in.at[k],
            device_id={"frame": 2 * to + core}, device_id_type=MESH))
        scatter[-1].start()
    parts[chip] = mine[chunk(chip), :]
    recv[me] = send[me]
    for copy in scatter:
        copy.wait_recv()
    whole = parts[0]
    for k in range(1, chips):
        whole = whole + parts[k]
    sums[core, chunk(chip), :] = whole
    gather = []
    for k in range(1, chips):
        to = lax.rem(chip + k, chips)
        gather.append(pltpu.make_async_remote_copy(
            sums.at[core, chunk(chip)], sums.at[core, chunk(chip)], sum_out.at[k], sum_in.at[k],
            device_id={"frame": 2 * to + core}, device_id_type=MESH))
        gather[-1].start()
    forward = []
    for k in range(chips):
        from_chip = lax.rem(chip + chips - k, chips)
        if k:
            gather[k - 1].wait_recv()
        forward.append(pltpu.make_async_remote_copy(
            sums.at[core, chunk(from_chip)], sums.at[core, chunk(from_chip)], fwd_out.at[k], fwd_in.at[k],
            device_id={"frame": partner}, device_id_type=MESH))
        forward[-1].start()

    for copy in spread:
        copy.wait_recv()
    for k in range(FPB):
        rows = recv[:, k, :]
        ext_out[k, pl.ds(0, group, stride=2), :] = rows[:, 0:WPB]
        ext_out[k, pl.ds(1, group, stride=2), :] = pltpu.roll(rows, LANES // 2, 1)[:, 0:WPB]
    for copy in forward:
        copy.wait_recv()
    for k in range(FPB):
        for h in range(2):
            rows = sums[h, pl.ds(k, per_half, stride=FPB), :]
            for s in range(2):
                here = rows if s == 0 else pltpu.roll(rows, LANES // 2, 1)
                start = s * pairs + h * per_half
                coadd_out[k, start:start + per_half, :] = here[:, 0:WPB] / here[:, WPB:WPB + 1]
    down.wait_send()
    up.wait_send()
    swap_done = scatter + gather + forward + spread
    for copy in swap_done:
        copy.wait_send()


VMEM = pl.BlockSpec(memory_space=pltpu.VMEM)
SMEM = pl.BlockSpec(memory_space=pltpu.SMEM)
ANY = pl.BlockSpec(memory_space=pl.ANY)


def local(exposure, row_prof, col_prof, row_off, col_off, dest, fibre_weight):
    group = lax.axis_size("patch")
    frames = lax.axis_size("frame")
    count = dest.shape[1]
    chips = frames // 2
    f32, bf16 = jnp.float32, jnp.bfloat16
    _, channels, depth, width = exposure.shape
    tiles = width // LANES
    stride = -(-count // 8) * 8
    ext_out, coadd_out = pl.pallas_call(
        functools.partial(solve_kernel, count, group, frames),
        out_shape=(
            jax.ShapeDtypeStruct((FPB, 2 * group, WPB), f32),
            jax.ShapeDtypeStruct((FPB, count, WPB), f32),
        ),
        in_specs=[SMEM] * 3 + [ANY] * 4,
        out_specs=(VMEM, VMEM),
        scratch_shapes=[
            pltpu.VMEM((channels, depth, width), bf16),
            pltpu.VMEM((count, WPB, PR), bf16),
            pltpu.VMEM((FPB, count, PC), bf16),
            pltpu.VMEM((count, FPB), f32),
            pltpu.VMEM((channels, HALO, width), bf16),
            pltpu.VMEM((channels, HALO, width), bf16),
            pltpu.VMEM((channels, tiles + 1, PR + HALO, LANES), f32),
            pltpu.VMEM((2, FPB * stride, LANES), f32),
            pltpu.VMEM((count, PR, LANES), bf16),
            pltpu.VMEM((count, 32, PC), bf16),
            pltpu.VMEM((count, 2, PR + HALO, LANES), f32),
            pltpu.VMEM((count, 2, PR + HALO, LANES), f32),
            pltpu.VMEM((count, PR, PC), f32),
            pltpu.VMEM((count, 32, LANES), f32),
            pltpu.VMEM((count, 32, LANES), f32),
            pltpu.VMEM((count + 1, 32, LANES), f32),
            pltpu.VMEM((count, 8, LANES), f32),
            pltpu.VMEM((group, FPB, LANES), f32),
            pltpu.VMEM((group, FPB, LANES), f32),
            pltpu.VMEM((2, LANES, LANES), f32),
            pltpu.VMEM((LANES, LANES), f32),
            pltpu.VMEM((LANES, LANES), f32),
            pltpu.VMEM((chips, 32, LANES), f32),
            pltpu.VMEM((2, LANES, LANES), f32),
            pltpu.SemaphoreType.DMA((4,)),
            pltpu.SemaphoreType.DMA((2,)),
            pltpu.SemaphoreType.DMA((2,)),
            pltpu.SemaphoreType.DMA((2,)),
            pltpu.SemaphoreType.DMA((group,)),
            pltpu.SemaphoreType.DMA((group,)),
            pltpu.SemaphoreType.DMA((chips,)),
            pltpu.SemaphoreType.DMA((chips,)),
            pltpu.SemaphoreType.DMA((chips,)),
            pltpu.SemaphoreType.DMA((chips,)),
            pltpu.SemaphoreType.DMA((chips,)),
            pltpu.SemaphoreType.DMA((chips,)),
        ],
        compiler_params=pltpu.CompilerParams(
            collective_id=0, has_side_effects=True, vmem_limit_bytes=48 << 20),
        name="solve",
    )(
        row_off[0], col_off[0], dest[0], exposure[0], row_prof[0],
        jnp.swapaxes(col_prof[0], 0, 1), fibre_weight[0],
    )
    return jnp.transpose(ext_out, (1, 2, 0))[None], jnp.transpose(coadd_out, (1, 2, 0))


def solution(mesh):
    in_specs = (
        P("frame", None, ("section", "patch"), None),
        P("frame", ("section", "patch"), None, None),
        P("frame", ("section", "patch"), None, None),
        P("frame", ("section", "patch")),
        P("frame", ("section", "patch")),
        P("frame", ("section", "patch")),
        P("frame", ("section", "patch"), None),
    )
    out_specs = (P("frame", ("section", "patch"), None, None), P(("section", "patch"), None, None))
    return jax.shard_map(local, mesh=mesh, in_specs=in_specs, out_specs=out_specs, check_vma=False)
```

```python
import functools

import jax
import jax.numpy as jnp
from jax import lax
from jax.experimental import pallas as pl
from jax.experimental.pallas import tpu as pltpu
from jax.sharding import PartitionSpec as P

HALO = 8
PC = 256
ITERS = 6
PR = 64
LANES = 128
WPB = 50
FPB = 25
MESH = pl.DeviceIdType.MESH
NT = (((1,), (1,)), ((), ()))


def lane_index(shape):
    return lax.broadcasted_iota(jnp.int32, shape, len(shape) - 1)


def second_piece(value, first):
    head = value.astype(jnp.bfloat16).astype(jnp.float32)
    return jnp.where(first, value, value - head).astype(jnp.bfloat16)


def project(weighted, cols, profile, half):
    head = [g.astype(jnp.bfloat16) for g in weighted]
    tail = [(g - h.astype(jnp.float32)).astype(jnp.bfloat16) for g, h in zip(weighted, head)]
    both = [jnp.concatenate([h, t], axis=0) for h, t in zip(head, tail)]
    folded = [
        lax.dot_general(c, g, NT, preferred_element_type=jnp.float32) for c, g in zip(cols, both)
    ]
    folded = [f + pltpu.roll(f, LANES // 2, 1) for f in folded]
    pieces = [second_piece(f, half) for f in folded]
    return [
        jnp.dot(f, jnp.concatenate([r, r], axis=0), preferred_element_type=jnp.float32)
        for f, r in zip(pieces, profile)
    ]


def image_of(direction, cols, profile, half, quarter):
    pieces = [second_piece(d, half) for d in direction]
    pieces = [jnp.concatenate([d, d], axis=0) for d in pieces]
    across = [
        lax.dot_general(r, d, NT, preferred_element_type=jnp.float32) for r, d in zip(profile, pieces)
    ]
    pieces = [second_piece(u, quarter) for u in across]
    return [
        jnp.dot(u, jnp.concatenate([c, c], axis=0), preferred_element_type=jnp.float32)
        for u, c in zip(pieces, cols)
    ]


def total(value):
    return jnp.sum(jnp.sum(value, axis=0, keepdims=True), axis=1, keepdims=True)


def solve_kernel(
    count, group, frames,
    row_hbm, col_hbm, dest_hbm, exposure, row_prof, col_prof, fibre_weight,
    ext_out, coadd_out,
    row_off, col_off, dest,
    pixels, rows_raw, cols_raw, weight_raw, low, high, ext, cols_wide, profile, cols,
    cut_weight, cut_value, inverse, direction, residual, spectra, norms, send, recv, contrib,
    arrived, mine, parts, sums,
    load_sem, halo_out, halo_in, swap_sem, out_sem, in_sem, part_out, part_in, sum_out, sum_in, fwd_out, fwd_in,
):
    f32 = jnp.float32
    section = lax.axis_index("section")
    frame = lax.axis_index("frame")
    me = lax.axis_index("patch")
    sections = lax.axis_size("section")
    core = lax.rem(frame, 2)
    chip = frame // 2
    chips = frames // 2
    partner = frame + 1 - 2 * core
    band = section * group + me
    bands = sections * group
    above = lax.rem(band + bands - 1, bands)
    below = lax.rem(band + 1, bands)

    def at_band(index):
        return {"section": index // group, "patch": lax.rem(index, group)}

    barrier = pltpu.get_barrier_semaphore()
    inner = [{"patch": lax.rem(me + k, group)} for k in range(1, group)]
    peers = [{"frame": lax.rem(frame + 2 * k, frames)} for k in range(1, chips)]
    partners = [at_band(above), at_band(below)] + [{"frame": partner}] + peers + inner
    for device in partners:
        pl.semaphore_signal(barrier, inc=1, device_id=device, device_id_type=MESH)
    loads = [
        pltpu.make_async_copy(source, target, load_sem.at[i])
        for i, (source, target) in enumerate(
            [
                (exposure, pixels), (row_prof, rows_raw), (col_prof, cols_raw), (fibre_weight, weight_raw),
                (row_hbm, row_off), (col_hbm, col_off), (dest_hbm, dest),
            ]
        )
    ]
    for load in loads:
        load.start()
    pl.semaphore_wait(barrier, len(partners))

    depth = exposure.shape[1]
    down = pltpu.make_async_remote_copy(
        exposure.at[:, depth - HALO:depth, :], low, halo_out.at[0], halo_in.at[0],
        device_id=at_band(below), device_id_type=MESH)
    up = pltpu.make_async_remote_copy(
        exposure.at[:, 0:HALO, :], high, halo_out.at[1], halo_in.at[1],
        device_id=at_band(above), device_id_type=MESH)
    down.start()
    up.start()

    half = lane_index((32, LANES)) < LANES // 2
    quarter = lane_index((PR, PR)) < PR // 2
    tiles = exposure.shape[2] // LANES

    loads[1].wait()
    for p in range(count):
        turned = jnp.pad(rows_raw[p].astype(f32), ((0, PR - WPB), (0, LANES - PR))).T[0:PR]
        profile[p] = jnp.concatenate([turned, turned], axis=1).astype(jnp.bfloat16)
    loads[2].wait()
    stride = cols_wide.shape[1] // FPB
    for k in range(FPB):
        for j in range(2):
            cols_wide[j, k * stride:k * stride + count, :] = (
                cols_raw[k, :, j * LANES:(j + 1) * LANES].astype(f32))
    gap = jnp.zeros((32 - FPB, PC), f32)
    for p in range(count):
        taken = [cols_wide[j, pl.ds(p, FPB, stride=stride), :] for j in range(2)]
        cols[p] = jnp.concatenate([jnp.concatenate(taken, axis=1), gap], axis=0).astype(jnp.bfloat16)

    loads[0].wait()
    for load in loads[3:]:
        load.wait()
    for channel in range(2):
        for tile in range(tiles):
            at = slice(tile * LANES, (tile + 1) * LANES)
            ext[channel, tile, HALO:PR, :] = pixels[channel, :, at].astype(f32)

    raw = jnp.concatenate([weight_raw[:, 0, :], jnp.zeros((count, LANES - FPB), f32)], axis=1)
    weights = jnp.concatenate([raw, jnp.zeros((LANES - count, LANES), f32)], axis=0).T[0:32]

    source = []
    for d in range(group):
        first = jnp.int32(count)
        last = jnp.int32(count)
        for p in range(count):
            last = jnp.where(dest[0, p] == d, p, last)
            first = jnp.where(dest[0, count - 1 - p] == d, count - 1 - p, first)
        source.append((first, jnp.where(last == first, count, last)))

    starts = [row_off[0, p] for p in range(count)]
    columns = [col_off[0, p] for p in range(count)]
    firsts = [c // LANES for c in columns]
    shifts = [c - t * LANES for c, t in zip(columns, firsts)]

    def cut(first, size):
        lanes = lane_index((size, LANES))
        for p in range(count):
            keep = lanes < LANES - shifts[p]
            moved = [
                [
                    pltpu.roll(ext[channel, firsts[p] + j, first:first + size, :], LANES - shifts[p], 1)
                    for j in range(3)
                ]
                for channel in range(2)
            ]
            for j in range(2):
                value, weight = [jnp.where(keep, m[j], m[j + 1]) for m in moved]
                cut_weight[p, j, first:first + size, :] = weight
                cut_value[p, j, first:first + size, :] = weight * value

    cut(HALO, PR - HALO)
    down.wait_recv()
    up.wait_recv()
    for channel in range(2):
        for tile in range(tiles):
            at = slice(tile * LANES, (tile + 1) * LANES)
            ext[channel, tile, 0:HALO, :] = jnp.where(band > 0, low[channel, :, at].astype(f32), 0.0)
            ext[channel, tile, PR:PR + HALO, :] = jnp.where(
                band < bands - 1, high[channel, :, at].astype(f32), 0.0)
    cut(0, HALO)
    cut(PR, HALO)

    every = list(range(count))
    c = [cols[p] for p in every]
    r = [profile[p] for p in every]
    weighted = []
    for p in every:
        inverse[p] = jnp.concatenate([cut_weight[p, j, pl.ds(starts[p], PR), :] for j in range(2)], axis=1)
        weighted.append(
            jnp.concatenate([cut_value[p, j, pl.ds(starts[p], PR), :] for j in range(2)], axis=1))
    for p, value in zip(every, project(weighted, c, r, half)):
        direction[p] = value
        residual[p] = value
        spectra[p] = jnp.zeros_like(value)
        norms[p] = jnp.broadcast_to(total(value * value), (8, LANES))
    spectra[count] = jnp.zeros((32, LANES), f32)

    def sweep(index, carry):
        c = [cols[p] for p in every]
        r = [profile[p] for p in every]
        along = [direction[p] for p in every]
        modeled = image_of(along, c, r, half, quarter)
        imaged = project([inverse[p] * m for p, m in zip(every, modeled)], c, r, half)
        curvature = [total(d * q) for d, q in zip(along, imaged)]
        now = [norms[p][0:1, 0:1] for p in every]
        size = [n / jnp.where(k > 0.0, k, 1.0) for n, k in zip(now, curvature)]
        left = [residual[p] - a * q for p, a, q in zip(every, size, imaged)]
        later = [total(e * e) for e in left]
        ratio = [n / jnp.where(b > 0.0, b, 1.0) for n, b in zip(later, now)]
        for p, a, d, e, n, k in zip(every, size, along, left, later, ratio):
            spectra[p] += a * d
            residual[p] = e
            norms[p] = jnp.broadcast_to(n, (8, LANES))
            direction[p] = e + k * d
        return carry

    lax.fori_loop(0, ITERS - 1, sweep, 0)
    along = [direction[p] for p in every]
    modeled = image_of(along, [cols[p] for p in every], [profile[p] for p in every], half, quarter)
    curvature = [
        2.0 * total(jnp.sum(inverse[p] * m * m, axis=0, keepdims=True)) for p, m in zip(every, modeled)
    ]
    for p, d, k in zip(every, along, curvature):
        spectra[p] += norms[p][0:1, 0:1] / jnp.where(k > 0.0, k, 1.0) * d

    pairs = count // 2
    per_half = pairs // 2
    marked = lane_index((32, LANES)) % (LANES // 2) == WPB
    for j in range(pairs):
        scale = jnp.where(
            half,
            jnp.broadcast_to(weights[:, j:j + 1], (32, LANES)),
            jnp.broadcast_to(weights[:, pairs + j:pairs + j + 1], (32, LANES)))
        value = scale * jnp.where(marked, 1.0, jnp.where(half, spectra[j], spectra[pairs + j]))
        start = (j % per_half) * FPB
        contrib[j // per_half, start:start + FPB, :] = value[0:FPB]
    for h in range(2):
        contrib[h, per_half * FPB:, :] = jnp.zeros((LANES - per_half * FPB, LANES), f32)
    swap = pltpu.make_async_remote_copy(
        contrib.at[1 - core], arrived, swap_sem.at[0], swap_sem.at[1],
        device_id={"frame": partner}, device_id_type=MESH)
    swap.start()
    for d in range(group):
        send[d] = jnp.where(half, spectra[source[d][0]], spectra[source[d][1]])[0:FPB]
    spread = []
    for k in range(1, group):
        to = lax.rem(me + k, group)
        spread.append(pltpu.make_async_remote_copy(
            send.at[to], recv.at[me], out_sem.at[k], in_sem.at[k],
            device_id={"patch": to}, device_id_type=MESH))
        spread[-1].start()

    def chunk(index):
        return pl.ds(pl.multiple_of(index * 32, 32), 32)

    swap.wait()
    mine[...] = contrib[core] + arrived[...]
    scatter = []
    for k in range(1, chips):
        to = lax.rem(chip + k, chips)
        scatter.append(pltpu.make_async_remote_copy(
            mine.at[chunk(to)], parts.at[chip], part_out.at[k], part_in.at[k],
            device_id={"frame": 2 * to + core}, device_id_type=MESH))
        scatter[-1].start()
    parts[chip] = mine[chunk(chip), :]
    recv[me] = send[me]
    for copy in scatter:
        copy.wait_recv()
    whole = parts[0]
    for k in range(1, chips):
        whole = whole + parts[k]
    sums[core, chunk(chip), :] = whole
    gather = []
    for k in range(1, chips):
        to = lax.rem(chip + k, chips)
        gather.append(pltpu.make_async_remote_copy(
            sums.at[core, chunk(chip)], sums.at[core, chunk(chip)], sum_out.at[k], sum_in.at[k],
            device_id={"frame": 2 * to + core}, device_id_type=MESH))
        gather[-1].start()
    forward = []
    for k in range(chips):
        from_chip = lax.rem(chip + chips - k, chips)
        if k:
            gather[k - 1].wait_recv()
        forward.append(pltpu.make_async_remote_copy(
            sums.at[core, chunk(from_chip)], sums.at[core, chunk(from_chip)], fwd_out.at[k], fwd_in.at[k],
            device_id={"frame": partner}, device_id_type=MESH))
        forward[-1].start()

    for copy in spread:
        copy.wait_recv()
    for k in range(FPB):
        rows = recv[:, k, :]
        ext_out[k, pl.ds(0, group, stride=2), :] = rows[:, 0:WPB]
        ext_out[k, pl.ds(1, group, stride=2), :] = pltpu.roll(rows, LANES // 2, 1)[:, 0:WPB]
    for copy in forward:
        copy.wait_recv()
    for k in range(FPB):
        for h in range(2):
            rows = sums[h, pl.ds(k, per_half, stride=FPB), :]
            for s in range(2):
                here = rows if s == 0 else pltpu.roll(rows, LANES // 2, 1)
                start = s * pairs + h * per_half
                coadd_out[k, start:start + per_half, :] = here[:, 0:WPB] / here[:, WPB:WPB + 1]
    down.wait_send()
    up.wait_send()
    swap_done = scatter + gather + forward + spread
    for copy in swap_done:
        copy.wait_send()


VMEM = pl.BlockSpec(memory_space=pltpu.VMEM)
SMEM = pl.BlockSpec(memory_space=pltpu.SMEM)
HBM = pl.BlockSpec(memory_space=pltpu.HBM)


def local(exposure, row_prof, col_prof, row_off, col_off, dest, fibre_weight):
    group = lax.axis_size("patch")
    frames = lax.axis_size("frame")
    count = dest.shape[1]
    chips = frames // 2
    f32, bf16 = jnp.float32, jnp.bfloat16
    _, channels, depth, width = exposure.shape
    tiles = width // LANES
    stride = -(-count // 8) * 8
    ext_out, coadd_out = pl.pallas_call(
        functools.partial(solve_kernel, count, group, frames),
        out_shape=(
            jax.ShapeDtypeStruct((FPB, 2 * group, WPB), f32),
            jax.ShapeDtypeStruct((FPB, count, WPB), f32),
        ),
        in_specs=[HBM] * 7,
        out_specs=(VMEM, VMEM),
        scratch_shapes=[
            pltpu.SMEM((1, count), jnp.int32),
            pltpu.SMEM((1, count), jnp.int32),
            pltpu.SMEM((1, count), jnp.int32),
            pltpu.VMEM((channels, depth, width), bf16),
            pltpu.VMEM((count, WPB, PR), bf16),
            pltpu.VMEM((FPB, count, PC), bf16),
            pltpu.VMEM((count, 1, FPB), f32),
            pltpu.VMEM((channels, HALO, width), bf16),
            pltpu.VMEM((channels, HALO, width), bf16),
            pltpu.VMEM((channels, tiles + 1, PR + HALO, LANES), f32),
            pltpu.VMEM((2, FPB * stride, LANES), f32),
            pltpu.VMEM((count, PR, LANES), bf16),
            pltpu.VMEM((count, 32, PC), bf16),
            pltpu.VMEM((count, 2, PR + HALO, LANES), f32),
            pltpu.VMEM((count, 2, PR + HALO, LANES), f32),
            pltpu.VMEM((count, PR, PC), f32),
            pltpu.VMEM((count, 32, LANES), f32),
            pltpu.VMEM((count, 32, LANES), f32),
            pltpu.VMEM((count + 1, 32, LANES), f32),
            pltpu.VMEM((count, 8, LANES), f32),
            pltpu.VMEM((group, FPB, LANES), f32),
            pltpu.VMEM((group, FPB, LANES), f32),
            pltpu.VMEM((2, LANES, LANES), f32),
            pltpu.VMEM((LANES, LANES), f32),
            pltpu.VMEM((LANES, LANES), f32),
            pltpu.VMEM((chips, 32, LANES), f32),
            pltpu.VMEM((2, LANES, LANES), f32),
            pltpu.SemaphoreType.DMA((7,)),
            pltpu.SemaphoreType.DMA((2,)),
            pltpu.SemaphoreType.DMA((2,)),
            pltpu.SemaphoreType.DMA((2,)),
            pltpu.SemaphoreType.DMA((group,)),
            pltpu.SemaphoreType.DMA((group,)),
            pltpu.SemaphoreType.DMA((chips,)),
            pltpu.SemaphoreType.DMA((chips,)),
            pltpu.SemaphoreType.DMA((chips,)),
            pltpu.SemaphoreType.DMA((chips,)),
            pltpu.SemaphoreType.DMA((chips,)),
            pltpu.SemaphoreType.DMA((chips,)),
        ],
        compiler_params=pltpu.CompilerParams(
            collective_id=0, has_side_effects=True, vmem_limit_bytes=48 << 20),
        name="solve",
    )(
        *[pltpu.with_memory_space_constraint(a, pltpu.HBM) for a in (row_off, col_off, dest, exposure[0], row_prof[0],
        jnp.swapaxes(col_prof[0], 0, 1), jnp.swapaxes(fibre_weight, 0, 1))],
    )
    return jnp.transpose(ext_out, (1, 2, 0))[None], jnp.transpose(coadd_out, (1, 2, 0))


def solution(mesh):
    in_specs = (
        P("frame", None, ("section", "patch"), None),
        P("frame", ("section", "patch"), None, None),
        P("frame", ("section", "patch"), None, None),
        P("frame", ("section", "patch")),
        P("frame", ("section", "patch")),
        P("frame", ("section", "patch")),
        P("frame", ("section", "patch"), None),
    )
    out_specs = (P("frame", ("section", "patch"), None, None), P(("section", "patch"), None, None))
    return jax.shard_map(local, mesh=mesh, in_specs=in_specs, out_specs=out_specs, check_vma=False)
```

```python
import functools

import jax
import jax.numpy as jnp
from jax import lax
from jax.experimental import pallas as pl
from jax.experimental.pallas import tpu as pltpu
from jax.sharding import PartitionSpec as P

HALO = 8
PC = 256
ITERS = 6
PR = 64
LANES = 128
WPB = 50
FPB = 25
SPREAD = 2
MESH = pl.DeviceIdType.MESH
NT = (((1,), (1,)), ((), ()))


def lane_index(shape):
    return lax.broadcasted_iota(jnp.int32, shape, len(shape) - 1)


def second_piece(value, first):
    head = value.astype(jnp.bfloat16).astype(jnp.float32)
    return jnp.where(first, value, value - head).astype(jnp.bfloat16)


def fold(weighted, cols):
    head = [g.astype(jnp.bfloat16) for g in weighted]
    tail = [(g - h.astype(jnp.float32)).astype(jnp.bfloat16) for g, h in zip(weighted, head)]
    return [
        lax.dot_general(c, jnp.concatenate([h, t], axis=0), NT, preferred_element_type=jnp.float32)
        for c, h, t in zip(cols, head, tail)
    ]


def unfold(folded, profile, half):
    folded = [f + pltpu.roll(f, LANES // 2, 1) for f in folded]
    pieces = [second_piece(f, half) for f in folded]
    return [
        jnp.dot(f, jnp.concatenate([r, r], axis=0), preferred_element_type=jnp.float32)
        for f, r in zip(pieces, profile)
    ]


def project(weighted, cols, profile, half):
    return unfold(fold(weighted, cols), profile, half)


def image_of(direction, cols, profile, half, quarter):
    pieces = [second_piece(d, half) for d in direction]
    pieces = [jnp.concatenate([d, d], axis=0) for d in pieces]
    across = [
        lax.dot_general(r, d, NT, preferred_element_type=jnp.float32) for r, d in zip(profile, pieces)
    ]
    pieces = [second_piece(u, quarter) for u in across]
    return [
        jnp.dot(u, jnp.concatenate([c, c], axis=0), preferred_element_type=jnp.float32)
        for u, c in zip(pieces, cols)
    ]


def total(value):
    return jnp.sum(jnp.sum(value, axis=0, keepdims=True), axis=1, keepdims=True)


def solve_kernel(
    count, group, frames,
    row_hbm, col_hbm, dest_hbm, exposure, row_prof, col_prof, fibre_weight,
    ext_out, coadd_out,
    row_off, col_off, dest,
    pixels, rows_raw, cols_raw, weight_raw, low, high, ext, cols_wide, profile, cols,
    cut_weight, cut_value, inverse, direction, residual, spectra, norms, send, recv, contrib,
    arrived, gathered, sums,
    load_sem, halo_out, halo_in, swap_out, swap_in, out_sem, in_sem, direct_out, direct_in, relay_out, relay_in,
    fwd_out, fwd_in,
):
    f32 = jnp.float32
    section = lax.axis_index("section")
    frame = lax.axis_index("frame")
    me = lax.axis_index("patch")
    sections = lax.axis_size("section")
    core = lax.rem(frame, 2)
    chip = frame // 2
    chips = frames // 2
    partner = frame + 1 - 2 * core
    band = section * group + me
    bands = sections * group
    above = lax.rem(band + bands - 1, bands)
    below = lax.rem(band + 1, bands)

    def at_band(index):
        return {"section": index // group, "patch": lax.rem(index, group)}

    barrier = pltpu.get_barrier_semaphore()
    inner = [{"patch": lax.rem(me + k, group)} for k in range(1, group)]
    peers = [{"frame": lax.rem(frame + step, frames)} for step in (2, frames - 2)]
    partners = [at_band(above), at_band(below)] + [{"frame": partner}] + peers + inner
    for device in partners:
        pl.semaphore_signal(barrier, inc=1, device_id=device, device_id_type=MESH)
    loads = [
        pltpu.make_async_copy(source, target, load_sem.at[i])
        for i, (source, target) in enumerate(
            [
                (exposure, pixels), (row_prof, rows_raw), (col_prof, cols_raw), (fibre_weight, weight_raw),
                (row_hbm, row_off), (col_hbm, col_off), (dest_hbm, dest),
            ]
        )
    ]
    for load in loads:
        load.start()
    pl.semaphore_wait(barrier, len(partners))

    depth = exposure.shape[1]
    down = pltpu.make_async_remote_copy(
        exposure.at[:, depth - HALO:depth, :], low, halo_out.at[0], halo_in.at[0],
        device_id=at_band(below), device_id_type=MESH)
    up = pltpu.make_async_remote_copy(
        exposure.at[:, 0:HALO, :], high, halo_out.at[1], halo_in.at[1],
        device_id=at_band(above), device_id_type=MESH)
    down.start()
    up.start()

    half = lane_index((32, LANES)) < LANES // 2
    quarter = lane_index((PR, PR)) < PR // 2
    tiles = exposure.shape[2] // LANES

    loads[1].wait()
    for p in range(count):
        turned = jnp.pad(rows_raw[p].astype(f32), ((0, PR - WPB), (0, LANES - PR))).T[0:PR]
        profile[p] = jnp.concatenate([turned, turned], axis=1).astype(jnp.bfloat16)
    loads[2].wait()
    stride = cols_wide.shape[1] // FPB
    for k in range(FPB):
        for j in range(2):
            cols_wide[j, k * stride:k * stride + count, :] = (
                cols_raw[k, :, j * LANES:(j + 1) * LANES].astype(f32))
    gap = jnp.zeros((32 - FPB, PC), f32)
    for p in range(count):
        taken = [cols_wide[j, pl.ds(p, FPB, stride=stride), :] for j in range(2)]
        cols[p] = jnp.concatenate([jnp.concatenate(taken, axis=1), gap], axis=0).astype(jnp.bfloat16)

    loads[0].wait()
    for load in loads[3:]:
        load.wait()
    for channel in range(2):
        for tile in range(tiles):
            at = slice(tile * LANES, (tile + 1) * LANES)
            ext[channel, tile, HALO:PR, :] = pixels[channel, :, at].astype(f32)

    raw = jnp.concatenate([weight_raw[:, 0, :], jnp.zeros((count, LANES - FPB), f32)], axis=1)
    weights = jnp.concatenate([raw, jnp.zeros((LANES - count, LANES), f32)], axis=0).T[0:32]

    source = []
    for d in range(group):
        first = jnp.int32(count)
        last = jnp.int32(count)
        for p in range(count):
            last = jnp.where(dest[0, p] == d, p, last)
            first = jnp.where(dest[0, count - 1 - p] == d, count - 1 - p, first)
        source.append((first, jnp.where(last == first, count, last)))

    starts = [row_off[0, p] for p in range(count)]
    columns = [col_off[0, p] for p in range(count)]
    firsts = [c // LANES for c in columns]
    shifts = [c - t * LANES for c, t in zip(columns, firsts)]

    def cut(first, size):
        lanes = lane_index((size, LANES))
        for p in range(count):
            keep = lanes < LANES - shifts[p]
            moved = [
                [
                    pltpu.roll(ext[channel, firsts[p] + j, first:first + size, :], LANES - shifts[p], 1)
                    for j in range(3)
                ]
                for channel in range(2)
            ]
            for j in range(2):
                value, weight = [jnp.where(keep, m[j], m[j + 1]) for m in moved]
                cut_weight[p, j, first:first + size, :] = weight
                cut_value[p, j, first:first + size, :] = weight * value

    cut(HALO, PR - HALO)
    down.wait_recv()
    up.wait_recv()
    for channel in range(2):
        for tile in range(tiles):
            at = slice(tile * LANES, (tile + 1) * LANES)
            ext[channel, tile, 0:HALO, :] = jnp.where(band > 0, low[channel, :, at].astype(f32), 0.0)
            ext[channel, tile, PR:PR + HALO, :] = jnp.where(
                band < bands - 1, high[channel, :, at].astype(f32), 0.0)
    cut(0, HALO)
    cut(PR, HALO)

    every = list(range(count))
    def begin(p):
        inverse[p] = jnp.concatenate([cut_weight[p, j, pl.ds(starts[p], PR), :] for j in range(2)], axis=1)
        value = jnp.concatenate([cut_value[p, j, pl.ds(starts[p], PR), :] for j in range(2)], axis=1)
        folded = fold([value], [cols[p]])
        yield
        rhs = unfold(folded, [profile[p]], half)[0]
        yield
        direction[p] = rhs
        residual[p] = rhs
        spectra[p] = jnp.zeros_like(rhs)
        norms[p] = jnp.broadcast_to(total(rhs * rhs), (8, LANES))
        yield

    def model(p):
        pieces = second_piece(direction[p], half)
        across = lax.dot_general(
            profile[p], jnp.concatenate([pieces, pieces], axis=0), NT, preferred_element_type=f32)
        yield
        pieces = second_piece(across, quarter)
        modeled = jnp.dot(pieces, jnp.concatenate([cols[p], cols[p]], axis=0), preferred_element_type=f32)
        yield
        return modeled

    def iterate(p):
        modeled = yield from model(p)
        folded = fold([inverse[p] * modeled], [cols[p]])
        yield
        imaged = unfold(folded, [profile[p]], half)[0]
        yield
        curvature = total(direction[p] * imaged)
        yield
        now = norms[p][0:1, 0:1]
        size = now / jnp.where(curvature > 0.0, curvature, 1.0)
        left = residual[p] - size * imaged
        residual[p] = left
        spectra[p] += size * direction[p]
        later = total(left * left)
        yield
        norms[p] = jnp.broadcast_to(later, (8, LANES))
        direction[p] = residual[p] + later / jnp.where(now > 0.0, now, 1.0) * direction[p]
        yield

    def conclude(p):
        modeled = yield from model(p)
        curvature = 2.0 * total(jnp.sum(inverse[p] * modeled * modeled, axis=0, keepdims=True))
        yield
        spectra[p] += norms[p][0:1, 0:1] / jnp.where(curvature > 0.0, curvature, 1.0) * direction[p]
        yield

    def emit(chain, spread):
        pending = {p: chain(p) for p in every}
        key = {p: p * spread for p in every}
        while pending:
            p = min(pending, key=lambda q: (key[q], q))
            key[p] += count
            try:
                next(pending[p])
            except StopIteration:
                del pending[p]

    def whole_chain(p):
        yield from begin(p)
        for _ in range(ITERS - 1):
            yield from iterate(p)
        yield from conclude(p)

    emit(whole_chain, SPREAD)
    spectra[count] = jnp.zeros((32, LANES), f32)

    blocks = [slice(0, LANES // 2), slice(LANES // 2, LANES)]
    pairs = count // 2
    per_half = pairs // 2
    marked = lane_index((32, LANES)) % (LANES // 2) == WPB
    for j in range(pairs):
        scale = jnp.where(
            half,
            jnp.broadcast_to(weights[:, j:j + 1], (32, LANES)),
            jnp.broadcast_to(weights[:, pairs + j:pairs + j + 1], (32, LANES)))
        value = scale * jnp.where(marked, 1.0, jnp.where(half, spectra[j], spectra[pairs + j]))
        start = (j % per_half) * FPB
        contrib[j // per_half, start:start + FPB, :] = value[0:FPB]
    for h in range(2):
        contrib[h, per_half * FPB:, :] = jnp.zeros((LANES - per_half * FPB, LANES), f32)
    swaps = [
        pltpu.make_async_remote_copy(
            contrib.at[1 - core, part], arrived.at[part], swap_out.at[i], swap_in.at[i],
            device_id={"frame": partner}, device_id_type=MESH)
        for i, part in enumerate(blocks)
    ]
    for copy in swaps:
        copy.start()
    for d in range(group):
        send[d] = jnp.where(half, spectra[source[d][0]], spectra[source[d][1]])[0:FPB]
    side = group // 2
    near = [lax.div(me, side) * side + lax.rem(me + k, side) for k in range(1, side)]
    far = [(1 - lax.div(me, side)) * side + lax.rem(me + k, side) for k in range(side)]
    spread = [
        pltpu.make_async_remote_copy(
            send.at[to], recv.at[me], out_sem.at[k], in_sem.at[k],
            device_id={"patch": to}, device_id_type=MESH)
        for k, to in enumerate(near + far)
    ]
    for copy in spread[:side - 1]:
        copy.start()

    after, before = lax.rem(chip + 1, chips), lax.rem(chip + chips - 1, chips)

    def pass_on(owner, part, forward, out_sem, in_sem):
        return pltpu.make_async_remote_copy(
            gathered.at[owner, part], gathered.at[owner, part], out_sem, in_sem,
            device_id={"frame": 2 * (after if forward else before) + core}, device_id_type=MESH)

    for copy, part in zip(swaps, blocks):
        copy.wait_recv()
        gathered[chip, part, :] = contrib[core, part, :] + arrived[part, :]
    ahead = [pass_on(chip, part, True, direct_out.at[i], direct_in.at[i]) for i, part in enumerate(blocks)]
    back = [
        pass_on(chip, part, False, direct_out.at[2 + i], direct_in.at[2 + i])
        for i, part in enumerate(blocks)
    ]
    for copy in (ahead[0], back[1], ahead[1], back[0]):
        copy.start()
    for copy in spread[side - 1:]:
        copy.start()
    recv[me] = send[me]
    ahead[0].wait_recv()
    relays = [pass_on(before, blocks[0], True, relay_out.at[0], relay_in.at[0])]
    relays[0].start()
    back[1].wait_recv()
    relays.append(pass_on(after, blocks[1], False, relay_out.at[1], relay_in.at[1]))
    relays[1].start()
    ahead[1].wait_recv()
    back[0].wait_recv()
    forward = []
    for i, part in enumerate(blocks):
        relays[i].wait_recv()
        whole = gathered[0, part, :]
        for k in range(1, chips):
            whole = whole + gathered[k, part, :]
        sums[core, part, :] = whole
        forward.append(pltpu.make_async_remote_copy(
            sums.at[core, part], sums.at[core, part], fwd_out.at[i], fwd_in.at[i],
            device_id={"frame": partner}, device_id_type=MESH))
        forward[i].start()

    for copy in spread:
        copy.wait_recv()
    for k in range(FPB):
        rows = recv[:, k, :]
        ext_out[k, pl.ds(0, group, stride=2), :] = rows[:, 0:WPB]
        ext_out[k, pl.ds(1, group, stride=2), :] = pltpu.roll(rows, LANES // 2, 1)[:, 0:WPB]
    for copy in forward:
        copy.wait_recv()
    for k in range(FPB):
        for h in range(2):
            rows = sums[h, pl.ds(k, per_half, stride=FPB), :]
            for s in range(2):
                here = rows if s == 0 else pltpu.roll(rows, LANES // 2, 1)
                start = s * pairs + h * per_half
                coadd_out[k, start:start + per_half, :] = here[:, 0:WPB] / here[:, WPB:WPB + 1]
    down.wait_send()
    up.wait_send()
    for copy in swaps + ahead + back + relays + forward + spread:
        copy.wait_send()


VMEM = pl.BlockSpec(memory_space=pltpu.VMEM)
SMEM = pl.BlockSpec(memory_space=pltpu.SMEM)
HBM = pl.BlockSpec(memory_space=pltpu.HBM)


def local(exposure, row_prof, col_prof, row_off, col_off, dest, fibre_weight):
    group = lax.axis_size("patch")
    frames = lax.axis_size("frame")
    count = dest.shape[1]
    chips = frames // 2
    f32, bf16 = jnp.float32, jnp.bfloat16
    _, channels, depth, width = exposure.shape
    tiles = width // LANES
    stride = -(-count // 8) * 8
    ext_out, coadd_out = pl.pallas_call(
        functools.partial(solve_kernel, count, group, frames),
        out_shape=(
            jax.ShapeDtypeStruct((FPB, 2 * group, WPB), f32),
            jax.ShapeDtypeStruct((FPB, count, WPB), f32),
        ),
        in_specs=[HBM] * 7,
        out_specs=(VMEM, VMEM),
        scratch_shapes=[
            pltpu.SMEM((1, count), jnp.int32),
            pltpu.SMEM((1, count), jnp.int32),
            pltpu.SMEM((1, count), jnp.int32),
            pltpu.VMEM((channels, depth, width), bf16),
            pltpu.VMEM((count, WPB, PR), bf16),
            pltpu.VMEM((FPB, count, PC), bf16),
            pltpu.VMEM((count, 1, FPB), f32),
            pltpu.VMEM((channels, HALO, width), bf16),
            pltpu.VMEM((channels, HALO, width), bf16),
            pltpu.VMEM((channels, tiles + 1, PR + HALO, LANES), f32),
            pltpu.VMEM((2, FPB * stride, LANES), f32),
            pltpu.VMEM((count, PR, LANES), bf16),
            pltpu.VMEM((count, 32, PC), bf16),
            pltpu.VMEM((count, 2, PR + HALO, LANES), f32),
            pltpu.VMEM((count, 2, PR + HALO, LANES), f32),
            pltpu.VMEM((count, PR, PC), f32),
            pltpu.VMEM((count, 32, LANES), f32),
            pltpu.VMEM((count, 32, LANES), f32),
            pltpu.VMEM((count + 1, 32, LANES), f32),
            pltpu.VMEM((count, 8, LANES), f32),
            pltpu.VMEM((group, FPB, LANES), f32),
            pltpu.VMEM((group, FPB, LANES), f32),
            pltpu.VMEM((2, LANES, LANES), f32),
            pltpu.VMEM((LANES, LANES), f32),
            pltpu.VMEM((chips, LANES, LANES), f32),
            pltpu.VMEM((2, LANES, LANES), f32),
            pltpu.SemaphoreType.DMA((7,)),
            pltpu.SemaphoreType.DMA((2,)),
            pltpu.SemaphoreType.DMA((2,)),
            pltpu.SemaphoreType.DMA((2,)),
            pltpu.SemaphoreType.DMA((2,)),
            pltpu.SemaphoreType.DMA((group,)),
            pltpu.SemaphoreType.DMA((group,)),
            pltpu.SemaphoreType.DMA((4,)),
            pltpu.SemaphoreType.DMA((4,)),
            pltpu.SemaphoreType.DMA((2,)),
            pltpu.SemaphoreType.DMA((2,)),
            pltpu.SemaphoreType.DMA((2,)),
            pltpu.SemaphoreType.DMA((2,)),
        ],
        compiler_params=pltpu.CompilerParams(
            collective_id=0, has_side_effects=True, vmem_limit_bytes=48 << 20),
        name="solve",
    )(
        *[pltpu.with_memory_space_constraint(a, pltpu.HBM) for a in (row_off, col_off, dest, exposure[0], row_prof[0],
        jnp.swapaxes(col_prof[0], 0, 1), jnp.swapaxes(fibre_weight, 0, 1))],
    )
    return jnp.transpose(ext_out, (1, 2, 0))[None], jnp.transpose(coadd_out, (1, 2, 0))


def solution(mesh):
    in_specs = (
        P("frame", None, ("section", "patch"), None),
        P("frame", ("section", "patch"), None, None),
        P("frame", ("section", "patch"), None, None),
        P("frame", ("section", "patch")),
        P("frame", ("section", "patch")),
        P("frame", ("section", "patch")),
        P("frame", ("section", "patch"), None),
    )
    out_specs = (P("frame", ("section", "patch"), None, None), P(("section", "patch"), None, None))
    return jax.shard_map(local, mesh=mesh, in_specs=in_specs, out_specs=out_specs, check_vma=False)
```

```python
import functools

import jax
import jax.numpy as jnp
from jax import lax
from jax.experimental import pallas as pl
from jax.experimental.pallas import tpu as pltpu
from jax.sharding import PartitionSpec as P

HALO = 8
PC = 256
ITERS = 6
PR = 64
LANES = 128
WPB = 50
FPB = 25
SPREAD = 2
MESH = pl.DeviceIdType.MESH
NT = (((1,), (1,)), ((), ()))


def lane_index(shape):
    return lax.broadcasted_iota(jnp.int32, shape, len(shape) - 1)


def second_piece(value, first):
    head = value.astype(jnp.bfloat16).astype(jnp.float32)
    return jnp.where(first, value, value - head).astype(jnp.bfloat16)


def fold(weighted, cols):
    head = [g.astype(jnp.bfloat16) for g in weighted]
    tail = [(g - h.astype(jnp.float32)).astype(jnp.bfloat16) for g, h in zip(weighted, head)]
    return [
        lax.dot_general(c, jnp.concatenate([h, t], axis=0), NT, preferred_element_type=jnp.float32)
        for c, h, t in zip(cols, head, tail)
    ]


def unfold(folded, profile, half):
    folded = [f + pltpu.roll(f, LANES // 2, 1) for f in folded]
    pieces = [second_piece(f, half) for f in folded]
    return [
        jnp.dot(f, jnp.concatenate([r, r], axis=0), preferred_element_type=jnp.float32)
        for f, r in zip(pieces, profile)
    ]


def project(weighted, cols, profile, half):
    return unfold(fold(weighted, cols), profile, half)


def image_of(direction, cols, profile, half, quarter):
    pieces = [second_piece(d, half) for d in direction]
    pieces = [jnp.concatenate([d, d], axis=0) for d in pieces]
    across = [
        lax.dot_general(r, d, NT, preferred_element_type=jnp.float32) for r, d in zip(profile, pieces)
    ]
    pieces = [second_piece(u, quarter) for u in across]
    return [
        jnp.dot(u, jnp.concatenate([c, c], axis=0), preferred_element_type=jnp.float32)
        for u, c in zip(pieces, cols)
    ]


def total(value):
    return jnp.sum(jnp.sum(value, axis=0, keepdims=True), axis=1, keepdims=True)


def solve_kernel(
    count, group, frames,
    row_hbm, col_hbm, dest_hbm, exposure, row_prof, col_prof, fibre_weight,
    ext_out, coadd_out,
    row_off, col_off, dest,
    pixels, rows_raw, cols_raw, weight_raw, low, high, ext, cols_wide, profile, cols,
    cut_weight, cut_value, inverse, direction, residual, spectra, norms, send, recv, contrib,
    arrived, gathered, sums,
    load_sem, halo_out, halo_in, swap_out, swap_in, out_sem, in_sem, direct_out, direct_in, relay_out, relay_in,
    fwd_out, fwd_in,
):
    f32 = jnp.float32
    section = lax.axis_index("section")
    frame = lax.axis_index("frame")
    me = lax.axis_index("patch")
    sections = lax.axis_size("section")
    core = lax.rem(frame, 2)
    chip = frame // 2
    chips = frames // 2
    partner = frame + 1 - 2 * core
    band = section * group + me
    bands = sections * group
    above = lax.rem(band + bands - 1, bands)
    below = lax.rem(band + 1, bands)

    def at_band(index):
        return {"section": index // group, "patch": lax.rem(index, group)}

    barrier = pltpu.get_barrier_semaphore()
    inner = [{"patch": lax.rem(me + k, group)} for k in range(1, group)]
    peers = [{"frame": lax.rem(frame + step, frames)} for step in (2, frames - 2)]
    partners = [at_band(above), at_band(below)] + [{"frame": partner}] + peers + inner
    for device in partners:
        pl.semaphore_signal(barrier, inc=1, device_id=device, device_id_type=MESH)
    loads = [
        pltpu.make_async_copy(source, target, load_sem.at[i])
        for i, (source, target) in enumerate(
            [
                (exposure, pixels), (row_prof, rows_raw), (col_prof, cols_raw), (fibre_weight, weight_raw),
                (row_hbm, row_off), (col_hbm, col_off), (dest_hbm, dest),
            ]
        )
    ]
    for load in loads:
        load.start()
    pl.semaphore_wait(barrier, len(partners))

    depth = exposure.shape[1]
    down = pltpu.make_async_remote_copy(
        exposure.at[:, depth - HALO:depth, :], low, halo_out.at[0], halo_in.at[0],
        device_id=at_band(below), device_id_type=MESH)
    up = pltpu.make_async_remote_copy(
        exposure.at[:, 0:HALO, :], high, halo_out.at[1], halo_in.at[1],
        device_id=at_band(above), device_id_type=MESH)
    down.start()
    up.start()

    half = lane_index((32, LANES)) < LANES // 2
    quarter = lane_index((PR, PR)) < PR // 2
    tiles = exposure.shape[2] // LANES

    loads[1].wait()
    for p in range(count):
        turned = jnp.pad(rows_raw[p].astype(f32), ((0, PR - WPB), (0, LANES - PR))).T[0:PR]
        profile[p] = jnp.concatenate([turned, turned], axis=1).astype(jnp.bfloat16)
    loads[2].wait()
    stride = cols_wide.shape[1] // FPB
    for k in range(FPB):
        for j in range(2):
            cols_wide[j, k * stride:k * stride + count, :] = (
                cols_raw[k, :, j * LANES:(j + 1) * LANES].astype(f32))
    gap = jnp.zeros((32 - FPB, PC), f32)
    for p in range(count):
        taken = [cols_wide[j, pl.ds(p, FPB, stride=stride), :] for j in range(2)]
        cols[p] = jnp.concatenate([jnp.concatenate(taken, axis=1), gap], axis=0).astype(jnp.bfloat16)

    loads[0].wait()
    for load in loads[3:]:
        load.wait()
    for channel in range(2):
        for tile in range(tiles):
            at = slice(tile * LANES, (tile + 1) * LANES)
            ext[channel, tile, HALO:PR, :] = pixels[channel, :, at].astype(f32)

    raw = jnp.concatenate([weight_raw[:, 0, :], jnp.zeros((count, LANES - FPB), f32)], axis=1)
    weights = jnp.concatenate([raw, jnp.zeros((LANES - count, LANES), f32)], axis=0).T[0:32]

    source = []
    for d in range(group):
        first = jnp.int32(count)
        last = jnp.int32(count)
        for p in range(count):
            last = jnp.where(dest[0, p] == d, p, last)
            first = jnp.where(dest[0, count - 1 - p] == d, count - 1 - p, first)
        source.append((first, jnp.where(last == first, count, last)))

    starts = [row_off[0, p] for p in range(count)]
    columns = [col_off[0, p] for p in range(count)]
    firsts = [c // LANES for c in columns]
    shifts = [c - t * LANES for c, t in zip(columns, firsts)]

    def cut(first, size):
        lanes = lane_index((size, LANES))
        for p in range(count):
            keep = lanes < LANES - shifts[p]
            moved = [
                [
                    pltpu.roll(ext[channel, firsts[p] + j, first:first + size, :], LANES - shifts[p], 1)
                    for j in range(3)
                ]
                for channel in range(2)
            ]
            for j in range(2):
                value, weight = [jnp.where(keep, m[j], m[j + 1]) for m in moved]
                cut_weight[p, j, first:first + size, :] = weight
                cut_value[p, j, first:first + size, :] = weight * value

    cut(HALO, PR - HALO)
    down.wait_recv()
    up.wait_recv()
    for channel in range(2):
        for tile in range(tiles):
            at = slice(tile * LANES, (tile + 1) * LANES)
            ext[channel, tile, 0:HALO, :] = jnp.where(band > 0, low[channel, :, at].astype(f32), 0.0)
            ext[channel, tile, PR:PR + HALO, :] = jnp.where(
                band < bands - 1, high[channel, :, at].astype(f32), 0.0)
    cut(0, HALO)
    cut(PR, HALO)

    every = list(range(count))
    def begin(p):
        inverse[p] = jnp.concatenate([cut_weight[p, j, pl.ds(starts[p], PR), :] for j in range(2)], axis=1)
        value = jnp.concatenate([cut_value[p, j, pl.ds(starts[p], PR), :] for j in range(2)], axis=1)
        folded = fold([value], [cols[p]])
        yield
        rhs = unfold(folded, [profile[p]], half)[0]
        yield
        direction[p] = rhs
        residual[p] = rhs
        spectra[p] = jnp.zeros_like(rhs)
        norms[p] = jnp.broadcast_to(total(rhs * rhs), (8, LANES))
        yield

    def model(p):
        pieces = second_piece(direction[p], half)
        across = lax.dot_general(
            profile[p], jnp.concatenate([pieces, pieces], axis=0), NT, preferred_element_type=f32)
        yield
        pieces = second_piece(across, quarter)
        modeled = jnp.dot(pieces, jnp.concatenate([cols[p], cols[p]], axis=0), preferred_element_type=f32)
        yield
        return modeled

    def iterate(p):
        modeled = yield from model(p)
        folded = fold([inverse[p] * modeled], [cols[p]])
        yield
        imaged = unfold(folded, [profile[p]], half)[0]
        yield
        curvature = total(direction[p] * imaged)
        yield
        now = norms[p][0:1, 0:1]
        size = now / jnp.where(curvature > 0.0, curvature, 1.0)
        left = residual[p] - size * imaged
        residual[p] = left
        spectra[p] += size * direction[p]
        later = total(left * left)
        yield
        norms[p] = jnp.broadcast_to(later, (8, LANES))
        direction[p] = residual[p] + later / jnp.where(now > 0.0, now, 1.0) * direction[p]
        yield

    def conclude(p):
        modeled = yield from model(p)
        curvature = 2.0 * total(jnp.sum(inverse[p] * modeled * modeled, axis=0, keepdims=True))
        yield
        spectra[p] += norms[p][0:1, 0:1] / jnp.where(curvature > 0.0, curvature, 1.0) * direction[p]
        yield

    def emit(chain, spread, order, hooks):
        pending = {p: chain(p) for p in order}
        key = {p: i * spread for i, p in enumerate(order)}
        while pending:
            p = min(pending, key=lambda q: (key[q], q))
            key[p] += count
            try:
                next(pending[p])
            except StopIteration:
                del pending[p]
            while hooks and not set(hooks[0][0]) & set(pending):
                hooks.pop(0)[1]()

    def whole_chain(p):
        yield from begin(p)
        for _ in range(ITERS - 1):
            yield from iterate(p)
        yield from conclude(p)

    pairs = count // 2
    per_half = pairs // 2
    marked = lane_index((32, LANES)) % (LANES // 2) == WPB
    blocks = [slice(0, LANES // 2), slice(LANES // 2, LANES)]
    cuts = [part.stop // FPB + 1 if part.stop < LANES else per_half for part in blocks]
    swaps = [
        pltpu.make_async_remote_copy(
            contrib.at[1 - core, part], arrived.at[part], swap_out.at[i], swap_in.at[i],
            device_id={"frame": partner}, device_id_type=MESH)
        for i, part in enumerate(blocks)
    ]

    def contribute(first, last, swap):
        for j in range(pairs):
            if not first <= j % per_half < last:
                continue
            scale = jnp.where(
                half,
                jnp.broadcast_to(weights[:, j:j + 1], (32, LANES)),
                jnp.broadcast_to(weights[:, pairs + j:pairs + j + 1], (32, LANES)))
            value = scale * jnp.where(marked, 1.0, jnp.where(half, spectra[j], spectra[pairs + j]))
            start = (j % per_half) * FPB
            contrib[j // per_half, start:start + FPB, :] = value[0:FPB]
        swap.start()

    for h in range(2):
        contrib[h, per_half * FPB:, :] = jnp.ones((LANES - per_half * FPB, LANES), f32)
    groups = [[p for p in every if p % per_half < cuts[0]], [p for p in every if p % per_half >= cuts[0]]]
    emit(whole_chain, SPREAD, groups[0] + groups[1], [
        (groups[0], lambda: contribute(0, cuts[0], swaps[0])),
        (groups[1], lambda: contribute(cuts[0], per_half, swaps[1])),
    ])
    spectra[count] = jnp.zeros((32, LANES), f32)

    for d in range(group):
        send[d] = jnp.where(half, spectra[source[d][0]], spectra[source[d][1]])[0:FPB]
    side = group // 2
    near = [lax.div(me, side) * side + lax.rem(me + k, side) for k in range(1, side)]
    far = [(1 - lax.div(me, side)) * side + lax.rem(me + k, side) for k in range(side)]
    spread = [
        pltpu.make_async_remote_copy(
            send.at[to], recv.at[me], out_sem.at[k], in_sem.at[k],
            device_id={"patch": to}, device_id_type=MESH)
        for k, to in enumerate(near + far)
    ]
    for copy in spread[:side - 1]:
        copy.start()

    after, before = lax.rem(chip + 1, chips), lax.rem(chip + chips - 1, chips)

    def pass_on(owner, part, forward, out_sem, in_sem):
        return pltpu.make_async_remote_copy(
            gathered.at[owner, part], gathered.at[owner, part], out_sem, in_sem,
            device_id={"frame": 2 * (after if forward else before) + core}, device_id_type=MESH)

    for copy, part in zip(swaps, blocks):
        copy.wait_recv()
        gathered[chip, part, :] = contrib[core, part, :] + arrived[part, :]
    ahead = [pass_on(chip, part, True, direct_out.at[i], direct_in.at[i]) for i, part in enumerate(blocks)]
    back = [
        pass_on(chip, part, False, direct_out.at[2 + i], direct_in.at[2 + i])
        for i, part in enumerate(blocks)
    ]
    for copy in (ahead[0], back[1], ahead[1], back[0]):
        copy.start()
    for copy in spread[side - 1:]:
        copy.start()
    recv[me] = send[me]
    ahead[0].wait_recv()
    relays = [pass_on(before, blocks[0], True, relay_out.at[0], relay_in.at[0])]
    relays[0].start()
    back[1].wait_recv()
    relays.append(pass_on(after, blocks[1], False, relay_out.at[1], relay_in.at[1]))
    relays[1].start()
    ahead[1].wait_recv()
    back[0].wait_recv()
    forward = []
    for i, part in enumerate(blocks):
        relays[i].wait_recv()
        whole = gathered[0, part, :]
        for k in range(1, chips):
            whole = whole + gathered[k, part, :]
        mass = jnp.where(
            lane_index(whole.shape) < LANES // 2,
            jnp.broadcast_to(whole[:, WPB:WPB + 1], whole.shape),
            jnp.broadcast_to(whole[:, LANES // 2 + WPB:LANES // 2 + WPB + 1], whole.shape))
        sums[core, part, :] = whole / mass
        forward.append(pltpu.make_async_remote_copy(
            sums.at[core, part], sums.at[core, part], fwd_out.at[i], fwd_in.at[i],
            device_id={"frame": partner}, device_id_type=MESH))
        forward[i].start()

    for copy in spread:
        copy.wait_recv()
    for k in range(FPB):
        rows = recv[:, k, :]
        ext_out[k, pl.ds(0, group, stride=2), :] = rows[:, 0:WPB]
        ext_out[k, pl.ds(1, group, stride=2), :] = pltpu.roll(rows, LANES // 2, 1)[:, 0:WPB]
    for copy in forward:
        copy.wait_recv()
    for k in range(FPB):
        for h in range(2):
            rows = sums[h, pl.ds(k, per_half, stride=FPB), :]
            for s in range(2):
                here = rows if s == 0 else pltpu.roll(rows, LANES // 2, 1)
                start = s * pairs + h * per_half
                coadd_out[k, start:start + per_half, :] = here[:, 0:WPB]
    down.wait_send()
    up.wait_send()
    for copy in swaps + ahead + back + relays + forward + spread:
        copy.wait_send()


def settle_kernel(ext_in, coadd_in, ext_out, coadd_out, sem):
    copies = [
        pltpu.make_async_copy(ext_in, ext_out, sem.at[0]),
        pltpu.make_async_copy(coadd_in, coadd_out, sem.at[1]),
    ]
    for copy in copies:
        copy.start()
    for copy in copies:
        copy.wait()


VMEM = pl.BlockSpec(memory_space=pltpu.VMEM)
SMEM = pl.BlockSpec(memory_space=pltpu.SMEM)
HBM = pl.BlockSpec(memory_space=pltpu.HBM)


def local(exposure, row_prof, col_prof, row_off, col_off, dest, fibre_weight):
    group = lax.axis_size("patch")
    frames = lax.axis_size("frame")
    count = dest.shape[1]
    chips = frames // 2
    f32, bf16 = jnp.float32, jnp.bfloat16
    _, channels, depth, width = exposure.shape
    tiles = width // LANES
    stride = -(-count // 8) * 8
    ext_out, coadd_out = pl.pallas_call(
        functools.partial(solve_kernel, count, group, frames),
        out_shape=(
            jax.ShapeDtypeStruct((FPB, 2 * group, WPB), f32),
            jax.ShapeDtypeStruct((FPB, count, WPB), f32),
        ),
        in_specs=[HBM] * 7,
        out_specs=(VMEM, VMEM),
        scratch_shapes=[
            pltpu.SMEM((1, count), jnp.int32),
            pltpu.SMEM((1, count), jnp.int32),
            pltpu.SMEM((1, count), jnp.int32),
            pltpu.VMEM((channels, depth, width), bf16),
            pltpu.VMEM((count, WPB, PR), bf16),
            pltpu.VMEM((FPB, count, PC), bf16),
            pltpu.VMEM((count, 1, FPB), f32),
            pltpu.VMEM((channels, HALO, width), bf16),
            pltpu.VMEM((channels, HALO, width), bf16),
            pltpu.VMEM((channels, tiles + 1, PR + HALO, LANES), f32),
            pltpu.VMEM((2, FPB * stride, LANES), f32),
            pltpu.VMEM((count, PR, LANES), bf16),
            pltpu.VMEM((count, 32, PC), bf16),
            pltpu.VMEM((count, 2, PR + HALO, LANES), f32),
            pltpu.VMEM((count, 2, PR + HALO, LANES), f32),
            pltpu.VMEM((count, PR, PC), f32),
            pltpu.VMEM((count, 32, LANES), f32),
            pltpu.VMEM((count, 32, LANES), f32),
            pltpu.VMEM((count + 1, 32, LANES), f32),
            pltpu.VMEM((count, 8, LANES), f32),
            pltpu.VMEM((group, FPB, LANES), f32),
            pltpu.VMEM((group, FPB, LANES), f32),
            pltpu.VMEM((2, LANES, LANES), f32),
            pltpu.VMEM((LANES, LANES), f32),
            pltpu.VMEM((chips, LANES, LANES), f32),
            pltpu.VMEM((2, LANES, LANES), f32),
            pltpu.SemaphoreType.DMA((7,)),
            pltpu.SemaphoreType.DMA((2,)),
            pltpu.SemaphoreType.DMA((2,)),
            pltpu.SemaphoreType.DMA((2,)),
            pltpu.SemaphoreType.DMA((2,)),
            pltpu.SemaphoreType.DMA((group,)),
            pltpu.SemaphoreType.DMA((group,)),
            pltpu.SemaphoreType.DMA((4,)),
            pltpu.SemaphoreType.DMA((4,)),
            pltpu.SemaphoreType.DMA((2,)),
            pltpu.SemaphoreType.DMA((2,)),
            pltpu.SemaphoreType.DMA((2,)),
            pltpu.SemaphoreType.DMA((2,)),
        ],
        compiler_params=pltpu.CompilerParams(
            collective_id=0, has_side_effects=True, vmem_limit_bytes=48 << 20),
        name="solve",
    )(
        *[pltpu.with_memory_space_constraint(a, pltpu.HBM) for a in (row_off, col_off, dest, exposure[0], row_prof[0],
        jnp.swapaxes(col_prof[0], 0, 1), jnp.swapaxes(fibre_weight, 0, 1))],
    )
    ext_out, coadd_out = pl.pallas_call(
        settle_kernel,
        out_shape=tuple(jax.ShapeDtypeStruct(a.shape, f32) for a in (ext_out, coadd_out)),
        in_specs=[VMEM] * 2,
        out_specs=(HBM, HBM),
        scratch_shapes=[pltpu.SemaphoreType.DMA((2,))],
        compiler_params=pltpu.CompilerParams(vmem_limit_bytes=8 << 20),
        name="settle",
    )(ext_out, coadd_out)
    return jnp.transpose(ext_out, (1, 2, 0))[None], jnp.transpose(coadd_out, (1, 2, 0))


def solution(mesh):
    in_specs = (
        P("frame", None, ("section", "patch"), None),
        P("frame", ("section", "patch"), None, None),
        P("frame", ("section", "patch"), None, None),
        P("frame", ("section", "patch")),
        P("frame", ("section", "patch")),
        P("frame", ("section", "patch")),
        P("frame", ("section", "patch"), None),
    )
    out_specs = (P("frame", ("section", "patch"), None, None), P(("section", "patch"), None, None))
    return jax.shard_map(local, mesh=mesh, in_specs=in_specs, out_specs=out_specs, check_vma=False)
```

```python
import functools

import jax
import jax.numpy as jnp
from jax import lax
from jax.experimental import pallas as pl
from jax.experimental.pallas import tpu as pltpu
from jax.sharding import PartitionSpec as P

HALO = 8
PC = 256
ITERS = 6
PR = 64
LANES = 128
WPB = 50
FPB = 25
SPREAD = 2
MESH = pl.DeviceIdType.MESH
NT = (((1,), (1,)), ((), ()))


def lane_index(shape):
    return lax.broadcasted_iota(jnp.int32, shape, len(shape) - 1)


def second_piece(value, first):
    head = value.astype(jnp.bfloat16).astype(jnp.float32)
    return jnp.where(first, value, value - head).astype(jnp.bfloat16)


def fold(weighted, cols):
    head = [g.astype(jnp.bfloat16) for g in weighted]
    tail = [(g - h.astype(jnp.float32)).astype(jnp.bfloat16) for g, h in zip(weighted, head)]
    return [
        lax.dot_general(c, jnp.concatenate([h, t], axis=0), NT, preferred_element_type=jnp.float32)
        for c, h, t in zip(cols, head, tail)
    ]


def unfold(folded, profile, half):
    folded = [f + pltpu.roll(f, LANES // 2, 1) for f in folded]
    pieces = [second_piece(f, half) for f in folded]
    return [
        jnp.dot(f, jnp.concatenate([r, r], axis=0), preferred_element_type=jnp.float32)
        for f, r in zip(pieces, profile)
    ]


def project(weighted, cols, profile, half):
    return unfold(fold(weighted, cols), profile, half)


def image_of(direction, cols, profile, half, quarter):
    pieces = [second_piece(d, half) for d in direction]
    pieces = [jnp.concatenate([d, d], axis=0) for d in pieces]
    across = [
        lax.dot_general(r, d, NT, preferred_element_type=jnp.float32) for r, d in zip(profile, pieces)
    ]
    pieces = [second_piece(u, quarter) for u in across]
    return [
        jnp.dot(u, jnp.concatenate([c, c], axis=0), preferred_element_type=jnp.float32)
        for u, c in zip(pieces, cols)
    ]


def total(value):
    return jnp.sum(jnp.sum(value, axis=0, keepdims=True), axis=1, keepdims=True)


def solve_kernel(
    count, group, frames,
    row_hbm, col_hbm, dest_hbm, exposure, row_prof, col_prof, fibre_weight,
    ext_out, coadd_out,
    row_off, col_off, dest,
    pixels, rows_raw, cols_raw, weight_raw, low, high, ext, cols_wide, profile, cols,
    cut_weight, cut_value, inverse, direction, residual, spectra, norms, send, recv, contrib,
    arrived, gathered, sums,
    load_sem, halo_out, halo_in, swap_out, swap_in, out_sem, in_sem, direct_out, direct_in, relay_out, relay_in,
    fwd_out, fwd_in,
):
    f32 = jnp.float32
    section = lax.axis_index("section")
    frame = lax.axis_index("frame")
    me = lax.axis_index("patch")
    sections = lax.axis_size("section")
    core = lax.rem(frame, 2)
    chip = frame // 2
    chips = frames // 2
    partner = frame + 1 - 2 * core
    band = section * group + me
    bands = sections * group
    above = lax.rem(band + bands - 1, bands)
    below = lax.rem(band + 1, bands)

    def at_band(index):
        return {"section": index // group, "patch": lax.rem(index, group)}

    barrier = pltpu.get_barrier_semaphore()
    inner = [{"patch": lax.rem(me + k, group)} for k in range(1, group)]
    peers = [{"frame": lax.rem(frame + step, frames)} for step in (2, frames - 2)]
    partners = [at_band(above), at_band(below)] + [{"frame": partner}] + peers + inner
    for device in partners:
        pl.semaphore_signal(barrier, inc=1, device_id=device, device_id_type=MESH)
    loads = [
        pltpu.make_async_copy(source, target, load_sem.at[i])
        for i, (source, target) in enumerate(
            [
                (exposure, pixels), (row_prof, rows_raw), (col_prof, cols_raw), (fibre_weight, weight_raw),
                (row_hbm, row_off), (col_hbm, col_off), (dest_hbm, dest),
            ]
        )
    ]
    for load in loads:
        load.start()
    pl.semaphore_wait(barrier, len(partners))

    depth = exposure.shape[1]
    down = pltpu.make_async_remote_copy(
        exposure.at[:, depth - HALO:depth, :], low, halo_out.at[0], halo_in.at[0],
        device_id=at_band(below), device_id_type=MESH)
    up = pltpu.make_async_remote_copy(
        exposure.at[:, 0:HALO, :], high, halo_out.at[1], halo_in.at[1],
        device_id=at_band(above), device_id_type=MESH)
    down.start()
    up.start()

    half = lane_index((32, LANES)) < LANES // 2
    quarter = lane_index((PR, PR)) < PR // 2
    tiles = exposure.shape[2] // LANES

    loads[1].wait()
    for p in range(count):
        turned = jnp.pad(rows_raw[p].astype(f32), ((0, PR - WPB), (0, LANES - PR))).T[0:PR]
        profile[p] = jnp.concatenate([turned, turned], axis=1).astype(jnp.bfloat16)
    loads[2].wait()
    stride = cols_wide.shape[1] // FPB
    for k in range(FPB):
        for j in range(2):
            cols_wide[j, k * stride:k * stride + count, :] = (
                cols_raw[k, :, j * LANES:(j + 1) * LANES].astype(f32))
    gap = jnp.zeros((32 - FPB, PC), f32)
    for p in range(count):
        taken = [cols_wide[j, pl.ds(p, FPB, stride=stride), :] for j in range(2)]
        cols[p] = jnp.concatenate([jnp.concatenate(taken, axis=1), gap], axis=0).astype(jnp.bfloat16)

    loads[0].wait()
    for load in loads[3:]:
        load.wait()
    for channel in range(2):
        for tile in range(tiles):
            at = slice(tile * LANES, (tile + 1) * LANES)
            ext[channel, tile, HALO:PR, :] = pixels[channel, :, at].astype(f32)

    raw = jnp.concatenate([weight_raw[:, 0, :], jnp.zeros((count, LANES - FPB), f32)], axis=1)
    weights = jnp.concatenate([raw, jnp.zeros((LANES - count, LANES), f32)], axis=0).T[0:32]

    source = []
    for d in range(group):
        first = jnp.int32(count)
        last = jnp.int32(count)
        for p in range(count):
            last = jnp.where(dest[0, p] == d, p, last)
            first = jnp.where(dest[0, count - 1 - p] == d, count - 1 - p, first)
        source.append((first, jnp.where(last == first, count, last)))

    starts = [row_off[0, p] for p in range(count)]
    columns = [col_off[0, p] for p in range(count)]
    firsts = [c // LANES for c in columns]
    shifts = [c - t * LANES for c, t in zip(columns, firsts)]

    def cut(first, size):
        lanes = lane_index((size, LANES))
        for p in range(count):
            keep = lanes < LANES - shifts[p]
            moved = [
                [
                    pltpu.roll(ext[channel, firsts[p] + j, first:first + size, :], LANES - shifts[p], 1)
                    for j in range(3)
                ]
                for channel in range(2)
            ]
            for j in range(2):
                value, weight = [jnp.where(keep, m[j], m[j + 1]) for m in moved]
                cut_weight[p, j, first:first + size, :] = weight
                cut_value[p, j, first:first + size, :] = weight * value

    cut(HALO, PR - HALO)
    down.wait_recv()
    up.wait_recv()
    for channel in range(2):
        for tile in range(tiles):
            at = slice(tile * LANES, (tile + 1) * LANES)
            ext[channel, tile, 0:HALO, :] = jnp.where(band > 0, low[channel, :, at].astype(f32), 0.0)
            ext[channel, tile, PR:PR + HALO, :] = jnp.where(
                band < bands - 1, high[channel, :, at].astype(f32), 0.0)
    cut(0, HALO)
    cut(PR, HALO)

    every = list(range(count))
    def begin(p):
        inverse[p] = jnp.concatenate([cut_weight[p, j, pl.ds(starts[p], PR), :] for j in range(2)], axis=1)
        value = jnp.concatenate([cut_value[p, j, pl.ds(starts[p], PR), :] for j in range(2)], axis=1)
        folded = fold([value], [cols[p]])
        yield
        rhs = unfold(folded, [profile[p]], half)[0]
        yield
        direction[p] = rhs
        residual[p] = rhs
        spectra[p] = jnp.zeros_like(rhs)
        norms[p] = jnp.broadcast_to(total(rhs * rhs), (8, LANES))
        yield

    def model(p):
        pieces = second_piece(direction[p], half)
        across = lax.dot_general(
            profile[p], jnp.concatenate([pieces, pieces], axis=0), NT, preferred_element_type=f32)
        yield
        pieces = second_piece(across, quarter)
        modeled = jnp.dot(pieces, jnp.concatenate([cols[p], cols[p]], axis=0), preferred_element_type=f32)
        yield
        return modeled

    def iterate(p):
        modeled = yield from model(p)
        folded = fold([inverse[p] * modeled], [cols[p]])
        yield
        imaged = unfold(folded, [profile[p]], half)[0]
        yield
        curvature = total(direction[p] * imaged)
        yield
        now = norms[p][0:1, 0:1]
        size = now / jnp.where(curvature > 0.0, curvature, 1.0)
        left = residual[p] - size * imaged
        residual[p] = left
        spectra[p] += size * direction[p]
        later = total(left * left)
        yield
        norms[p] = jnp.broadcast_to(later, (8, LANES))
        direction[p] = residual[p] + later / jnp.where(now > 0.0, now, 1.0) * direction[p]
        yield

    def conclude(p):
        modeled = yield from model(p)
        curvature = 2.0 * total(jnp.sum(inverse[p] * modeled * modeled, axis=0, keepdims=True))
        yield
        spectra[p] += norms[p][0:1, 0:1] / jnp.where(curvature > 0.0, curvature, 1.0) * direction[p]
        yield

    def emit(chain, spread, order, hooks):
        pending = {p: chain(p) for p in order}
        key = {p: i * spread for i, p in enumerate(order)}
        while pending:
            p = min(pending, key=lambda q: (key[q], q))
            key[p] += count
            try:
                next(pending[p])
            except StopIteration:
                del pending[p]
            while hooks and not set(hooks[0][0]) & set(pending):
                hooks.pop(0)[1]()

    def whole_chain(p):
        yield from begin(p)
        for _ in range(ITERS - 1):
            yield from iterate(p)
        yield from conclude(p)

    pairs = count // 2
    per_half = pairs // 2
    marked = lane_index((32, LANES)) % (LANES // 2) == WPB
    blocks = [slice(0, LANES // 2), slice(LANES // 2, LANES)]
    cuts = [part.stop // FPB + 1 if part.stop < LANES else per_half for part in blocks]
    swaps = [
        pltpu.make_async_remote_copy(
            contrib.at[1 - core, part], arrived.at[part], swap_out.at[i], swap_in.at[i],
            device_id={"frame": partner}, device_id_type=MESH)
        for i, part in enumerate(blocks)
    ]

    def contribute(first, last, swap):
        for j in range(pairs):
            if not first <= j % per_half < last:
                continue
            scale = jnp.where(
                half,
                jnp.broadcast_to(weights[:, j:j + 1], (32, LANES)),
                jnp.broadcast_to(weights[:, pairs + j:pairs + j + 1], (32, LANES)))
            value = scale * jnp.where(marked, 1.0, jnp.where(half, spectra[j], spectra[pairs + j]))
            start = (j % per_half) * FPB
            contrib[j // per_half, start:start + FPB, :] = value[0:FPB]
        swap.start()

    for h in range(2):
        contrib[h, per_half * FPB:, :] = jnp.ones((LANES - per_half * FPB, LANES), f32)
    groups = [[p for p in every if p % per_half < cuts[0]], [p for p in every if p % per_half >= cuts[0]]]
    emit(whole_chain, SPREAD, groups[0] + groups[1], [
        (groups[0], lambda: contribute(0, cuts[0], swaps[0])),
        (groups[1], lambda: contribute(cuts[0], per_half, swaps[1])),
    ])
    spectra[count] = jnp.zeros((32, LANES), f32)

    for d in range(group):
        send[d] = jnp.where(half, spectra[source[d][0]], spectra[source[d][1]])[0:FPB]
    side = group // 2
    near = [lax.div(me, side) * side + lax.rem(me + k, side) for k in range(1, side)]
    far = [(1 - lax.div(me, side)) * side + lax.rem(me + k, side) for k in range(side)]
    spread = [
        pltpu.make_async_remote_copy(
            send.at[to], recv.at[me], out_sem.at[k], in_sem.at[k],
            device_id={"patch": to}, device_id_type=MESH)
        for k, to in enumerate(far + near)
    ]
    for copy in spread[:side]:
        copy.start()

    after, before = lax.rem(chip + 1, chips), lax.rem(chip + chips - 1, chips)

    def pass_on(owner, part, forward, out_sem, in_sem):
        return pltpu.make_async_remote_copy(
            gathered.at[owner, part], gathered.at[owner, part], out_sem, in_sem,
            device_id={"frame": 2 * (after if forward else before) + core}, device_id_type=MESH)

    for copy, part in zip(swaps, blocks):
        copy.wait_recv()
        gathered[chip, part, :] = contrib[core, part, :] + arrived[part, :]
    ahead = [pass_on(chip, part, True, direct_out.at[i], direct_in.at[i]) for i, part in enumerate(blocks)]
    back = [
        pass_on(chip, part, False, direct_out.at[2 + i], direct_in.at[2 + i])
        for i, part in enumerate(blocks)
    ]
    for copy in (ahead[0], back[1], ahead[1], back[0]):
        copy.start()
    for copy in spread[side:]:
        copy.start()
    recv[me] = send[me]
    ahead[0].wait_recv()
    relays = [pass_on(before, blocks[0], True, relay_out.at[0], relay_in.at[0])]
    relays[0].start()
    back[1].wait_recv()
    relays.append(pass_on(after, blocks[1], False, relay_out.at[1], relay_in.at[1]))
    relays[1].start()
    ahead[1].wait_recv()
    back[0].wait_recv()
    forward = []
    for i, part in enumerate(blocks):
        relays[i].wait_recv()
        whole = gathered[0, part, :]
        for k in range(1, chips):
            whole = whole + gathered[k, part, :]
        mass = jnp.where(
            lane_index(whole.shape) < LANES // 2,
            jnp.broadcast_to(whole[:, WPB:WPB + 1], whole.shape),
            jnp.broadcast_to(whole[:, LANES // 2 + WPB:LANES // 2 + WPB + 1], whole.shape))
        sums[core, part, :] = whole / mass
        forward.append(pltpu.make_async_remote_copy(
            sums.at[core, part], sums.at[core, part], fwd_out.at[i], fwd_in.at[i],
            device_id={"frame": partner}, device_id_type=MESH))
        forward[i].start()

    for copy in spread:
        copy.wait_recv()
    for k in range(FPB):
        rows = recv[:, k, :]
        ext_out[k, pl.ds(0, group, stride=2), :] = rows[:, 0:WPB]
        ext_out[k, pl.ds(1, group, stride=2), :] = pltpu.roll(rows, LANES // 2, 1)[:, 0:WPB]
    for copy in forward:
        copy.wait_recv()
    for k in range(FPB):
        for h in range(2):
            rows = sums[h, pl.ds(k, per_half, stride=FPB), :]
            for s in range(2):
                here = rows if s == 0 else pltpu.roll(rows, LANES // 2, 1)
                start = s * pairs + h * per_half
                coadd_out[k, start:start + per_half, :] = here[:, 0:WPB]
    down.wait_send()
    up.wait_send()
    for copy in swaps + ahead + back + relays + forward + spread:
        copy.wait_send()


def settle_kernel(ext_in, coadd_in, ext_out, coadd_out, sem):
    copies = [
        pltpu.make_async_copy(ext_in, ext_out, sem.at[0]),
        pltpu.make_async_copy(coadd_in, coadd_out, sem.at[1]),
    ]
    for copy in copies:
        copy.start()
    for copy in copies:
        copy.wait()


VMEM = pl.BlockSpec(memory_space=pltpu.VMEM)
SMEM = pl.BlockSpec(memory_space=pltpu.SMEM)
HBM = pl.BlockSpec(memory_space=pltpu.HBM)


def local(exposure, row_prof, col_prof, row_off, col_off, dest, fibre_weight):
    group = lax.axis_size("patch")
    frames = lax.axis_size("frame")
    count = dest.shape[1]
    chips = frames // 2
    f32, bf16 = jnp.float32, jnp.bfloat16
    _, channels, depth, width = exposure.shape
    tiles = width // LANES
    stride = -(-count // 8) * 8
    ext_out, coadd_out = pl.pallas_call(
        functools.partial(solve_kernel, count, group, frames),
        out_shape=(
            jax.ShapeDtypeStruct((FPB, 2 * group, WPB), f32),
            jax.ShapeDtypeStruct((FPB, count, WPB), f32),
        ),
        in_specs=[HBM] * 7,
        out_specs=(VMEM, VMEM),
        scratch_shapes=[
            pltpu.SMEM((1, count), jnp.int32),
            pltpu.SMEM((1, count), jnp.int32),
            pltpu.SMEM((1, count), jnp.int32),
            pltpu.VMEM((channels, depth, width), bf16),
            pltpu.VMEM((count, WPB, PR), bf16),
            pltpu.VMEM((FPB, count, PC), bf16),
            pltpu.VMEM((count, 1, FPB), f32),
            pltpu.VMEM((channels, HALO, width), bf16),
            pltpu.VMEM((channels, HALO, width), bf16),
            pltpu.VMEM((channels, tiles + 1, PR + HALO, LANES), f32),
            pltpu.VMEM((2, FPB * stride, LANES), f32),
            pltpu.VMEM((count, PR, LANES), bf16),
            pltpu.VMEM((count, 32, PC), bf16),
            pltpu.VMEM((count, 2, PR + HALO, LANES), f32),
            pltpu.VMEM((count, 2, PR + HALO, LANES), f32),
            pltpu.VMEM((count, PR, PC), f32),
            pltpu.VMEM((count, 32, LANES), f32),
            pltpu.VMEM((count, 32, LANES), f32),
            pltpu.VMEM((count + 1, 32, LANES), f32),
            pltpu.VMEM((count, 8, LANES), f32),
            pltpu.VMEM((group, FPB, LANES), f32),
            pltpu.VMEM((group, FPB, LANES), f32),
            pltpu.VMEM((2, LANES, LANES), f32),
            pltpu.VMEM((LANES, LANES), f32),
            pltpu.VMEM((chips, LANES, LANES), f32),
            pltpu.VMEM((2, LANES, LANES), f32),
            pltpu.SemaphoreType.DMA((7,)),
            pltpu.SemaphoreType.DMA((2,)),
            pltpu.SemaphoreType.DMA((2,)),
            pltpu.SemaphoreType.DMA((2,)),
            pltpu.SemaphoreType.DMA((2,)),
            pltpu.SemaphoreType.DMA((group,)),
            pltpu.SemaphoreType.DMA((group,)),
            pltpu.SemaphoreType.DMA((4,)),
            pltpu.SemaphoreType.DMA((4,)),
            pltpu.SemaphoreType.DMA((2,)),
            pltpu.SemaphoreType.DMA((2,)),
            pltpu.SemaphoreType.DMA((2,)),
            pltpu.SemaphoreType.DMA((2,)),
        ],
        compiler_params=pltpu.CompilerParams(
            collective_id=0, has_side_effects=True, vmem_limit_bytes=48 << 20),
        name="solve",
    )(
        *[pltpu.with_memory_space_constraint(a, pltpu.HBM) for a in (row_off, col_off, dest, exposure[0], row_prof[0],
        jnp.swapaxes(col_prof[0], 0, 1), jnp.swapaxes(fibre_weight, 0, 1))],
    )
    ext_out, coadd_out = pl.pallas_call(
        settle_kernel,
        out_shape=tuple(jax.ShapeDtypeStruct(a.shape, f32) for a in (ext_out, coadd_out)),
        in_specs=[VMEM] * 2,
        out_specs=(HBM, HBM),
        scratch_shapes=[pltpu.SemaphoreType.DMA((2,))],
        compiler_params=pltpu.CompilerParams(vmem_limit_bytes=8 << 20),
        name="settle",
    )(ext_out, coadd_out)
    return jnp.transpose(ext_out, (1, 2, 0))[None], jnp.transpose(coadd_out, (1, 2, 0))


def solution(mesh):
    in_specs = (
        P("frame", None, ("section", "patch"), None),
        P("frame", ("section", "patch"), None, None),
        P("frame", ("section", "patch"), None, None),
        P("frame", ("section", "patch")),
        P("frame", ("section", "patch")),
        P("frame", ("section", "patch")),
        P("frame", ("section", "patch"), None),
    )
    out_specs = (P("frame", ("section", "patch"), None, None), P(("section", "patch"), None, None))
    return jax.shard_map(local, mesh=mesh, in_specs=in_specs, out_specs=out_specs, check_vma=False)
```

```python
import functools

import jax
import jax.numpy as jnp
from jax import lax
from jax.experimental import pallas as pl
from jax.experimental.pallas import tpu as pltpu
from jax.sharding import PartitionSpec as P

HALO = 8
PC = 256
ITERS = 6
PR = 64
LANES = 128
WPB = 50
FPB = 25
SPREAD = 2
MESH = pl.DeviceIdType.MESH
NT = (((1,), (1,)), ((), ()))


def lane_index(shape):
    return lax.broadcasted_iota(jnp.int32, shape, len(shape) - 1)


def second_piece(value, first):
    head = value.astype(jnp.bfloat16).astype(jnp.float32)
    return jnp.where(first, value, value - head).astype(jnp.bfloat16)


def fold(weighted, cols):
    head = [g.astype(jnp.bfloat16) for g in weighted]
    tail = [(g - h.astype(jnp.float32)).astype(jnp.bfloat16) for g, h in zip(weighted, head)]
    return [
        lax.dot_general(c, jnp.concatenate([h, t], axis=0), NT, preferred_element_type=jnp.float32)
        for c, h, t in zip(cols, head, tail)
    ]


def unfold(folded, profile, half):
    folded = [f + pltpu.roll(f, LANES // 2, 1) for f in folded]
    pieces = [second_piece(f, half) for f in folded]
    return [
        jnp.dot(f, jnp.concatenate([r, r], axis=0), preferred_element_type=jnp.float32)
        for f, r in zip(pieces, profile)
    ]


def project(weighted, cols, profile, half):
    return unfold(fold(weighted, cols), profile, half)


def image_of(direction, cols, profile, half, quarter):
    pieces = [second_piece(d, half) for d in direction]
    pieces = [jnp.concatenate([d, d], axis=0) for d in pieces]
    across = [
        lax.dot_general(r, d, NT, preferred_element_type=jnp.float32) for r, d in zip(profile, pieces)
    ]
    pieces = [second_piece(u, quarter) for u in across]
    return [
        jnp.dot(u, jnp.concatenate([c, c], axis=0), preferred_element_type=jnp.float32)
        for u, c in zip(pieces, cols)
    ]


def total(value):
    return jnp.sum(jnp.sum(value, axis=0, keepdims=True), axis=1, keepdims=True)


def solve_kernel(
    count, group, frames,
    row_hbm, col_hbm, dest_hbm, exposure, row_prof, col_prof, fibre_weight,
    ext_out, coadd_out,
    row_off, col_off, dest,
    pixels, rows_raw, cols_raw, weight_raw, low, high, ext, cols_wide, profile, cols,
    cut_weight, cut_value, inverse, direction, residual, spectra, norms, send, recv, contrib,
    arrived, gathered, sums,
    load_sem, halo_out, halo_in, swap_out, swap_in, out_sem, in_sem, direct_out, direct_in, relay_out, relay_in,
    fwd_out, fwd_in,
):
    f32 = jnp.float32
    section = lax.axis_index("section")
    frame = lax.axis_index("frame")
    me = lax.axis_index("patch")
    sections = lax.axis_size("section")
    core = lax.rem(frame, 2)
    chip = frame // 2
    chips = frames // 2
    partner = frame + 1 - 2 * core
    band = section * group + me
    bands = sections * group
    above = lax.rem(band + bands - 1, bands)
    below = lax.rem(band + 1, bands)

    def at_band(index):
        return {"section": index // group, "patch": lax.rem(index, group)}

    barrier = pltpu.get_barrier_semaphore()
    inner = [{"patch": lax.rem(me + k, group)} for k in range(1, group)]
    peers = [{"frame": lax.rem(frame + step, frames)} for step in (2, frames - 2)]
    partners = [at_band(above), at_band(below)] + [{"frame": partner}] + peers + inner
    for device in partners:
        pl.semaphore_signal(barrier, inc=1, device_id=device, device_id_type=MESH)
    loads = [
        pltpu.make_async_copy(source, target, load_sem.at[i])
        for i, (source, target) in enumerate(
            [
                (exposure, pixels), (row_prof, rows_raw), (col_prof, cols_raw), (fibre_weight, weight_raw),
                (row_hbm, row_off), (col_hbm, col_off), (dest_hbm, dest),
            ]
        )
    ]
    for load in loads:
        load.start()
    pl.semaphore_wait(barrier, len(partners))

    depth = exposure.shape[1]
    down = pltpu.make_async_remote_copy(
        exposure.at[:, depth - HALO:depth, :], low, halo_out.at[0], halo_in.at[0],
        device_id=at_band(below), device_id_type=MESH)
    up = pltpu.make_async_remote_copy(
        exposure.at[:, 0:HALO, :], high, halo_out.at[1], halo_in.at[1],
        device_id=at_band(above), device_id_type=MESH)
    down.start()
    up.start()

    half = lane_index((32, LANES)) < LANES // 2
    quarter = lane_index((PR, PR)) < PR // 2
    tiles = exposure.shape[2] // LANES

    loads[1].wait()
    for p in range(count):
        turned = jnp.pad(rows_raw[p].astype(f32), ((0, PR - WPB), (0, LANES - PR))).T[0:PR]
        profile[p] = jnp.concatenate([turned, turned], axis=1).astype(jnp.bfloat16)
    loads[2].wait()
    stride = cols_wide.shape[1] // FPB
    for k in range(FPB):
        for j in range(2):
            cols_wide[j, k * stride:k * stride + count, :] = (
                cols_raw[k, :, j * LANES:(j + 1) * LANES].astype(f32))
    gap = jnp.zeros((32 - FPB, PC), f32)
    for p in range(count):
        taken = [cols_wide[j, pl.ds(p, FPB, stride=stride), :] for j in range(2)]
        cols[p] = jnp.concatenate([jnp.concatenate(taken, axis=1), gap], axis=0).astype(jnp.bfloat16)

    loads[0].wait()
    for load in loads[3:]:
        load.wait()
    for channel in range(2):
        for tile in range(tiles):
            at = slice(tile * LANES, (tile + 1) * LANES)
            ext[channel, tile, HALO:PR, :] = pixels[channel, :, at].astype(f32)

    raw = jnp.concatenate([weight_raw[:, 0, :], jnp.zeros((count, LANES - FPB), f32)], axis=1)
    weights = jnp.concatenate([raw, jnp.zeros((LANES - count, LANES), f32)], axis=0).T[0:32]

    source = []
    for d in range(group):
        first = jnp.int32(count)
        last = jnp.int32(count)
        for p in range(count):
            last = jnp.where(dest[0, p] == d, p, last)
            first = jnp.where(dest[0, count - 1 - p] == d, count - 1 - p, first)
        source.append((first, jnp.where(last == first, count, last)))

    starts = [row_off[0, p] for p in range(count)]
    columns = [col_off[0, p] for p in range(count)]
    firsts = [c // LANES for c in columns]
    shifts = [c - t * LANES for c, t in zip(columns, firsts)]

    def cut(first, size):
        lanes = lane_index((size, LANES))
        for p in range(count):
            keep = lanes < LANES - shifts[p]
            moved = [
                [
                    pltpu.roll(ext[channel, firsts[p] + j, first:first + size, :], LANES - shifts[p], 1)
                    for j in range(3)
                ]
                for channel in range(2)
            ]
            for j in range(2):
                value, weight = [jnp.where(keep, m[j], m[j + 1]) for m in moved]
                cut_weight[p, j, first:first + size, :] = weight
                cut_value[p, j, first:first + size, :] = weight * value

    cut(HALO, PR - HALO)
    down.wait_recv()
    up.wait_recv()
    for channel in range(2):
        for tile in range(tiles):
            at = slice(tile * LANES, (tile + 1) * LANES)
            ext[channel, tile, 0:HALO, :] = jnp.where(band > 0, low[channel, :, at].astype(f32), 0.0)
            ext[channel, tile, PR:PR + HALO, :] = jnp.where(
                band < bands - 1, high[channel, :, at].astype(f32), 0.0)
    cut(0, HALO)
    cut(PR, HALO)

    every = list(range(count))
    def begin(p):
        inverse[p] = jnp.concatenate([cut_weight[p, j, pl.ds(starts[p], PR), :] for j in range(2)], axis=1)
        value = jnp.concatenate([cut_value[p, j, pl.ds(starts[p], PR), :] for j in range(2)], axis=1)
        folded = fold([value], [cols[p]])
        yield
        rhs = unfold(folded, [profile[p]], half)[0]
        yield
        direction[p] = rhs
        residual[p] = rhs
        spectra[p] = jnp.zeros_like(rhs)
        norms[p] = jnp.broadcast_to(total(rhs * rhs), (8, LANES))
        yield

    def model(p):
        pieces = second_piece(direction[p], half)
        across = lax.dot_general(
            profile[p], jnp.concatenate([pieces, pieces], axis=0), NT, preferred_element_type=f32)
        yield
        pieces = second_piece(across, quarter)
        modeled = jnp.dot(pieces, jnp.concatenate([cols[p], cols[p]], axis=0), preferred_element_type=f32)
        yield
        return modeled

    def iterate(p):
        modeled = yield from model(p)
        folded = fold([inverse[p] * modeled], [cols[p]])
        yield
        imaged = unfold(folded, [profile[p]], half)[0]
        yield
        curvature = total(direction[p] * imaged)
        yield
        now = norms[p][0:1, 0:1]
        size = now / jnp.where(curvature > 0.0, curvature, 1.0)
        left = residual[p] - size * imaged
        residual[p] = left
        spectra[p] += size * direction[p]
        later = total(left * left)
        yield
        norms[p] = jnp.broadcast_to(later, (8, LANES))
        direction[p] = residual[p] + later / jnp.where(now > 0.0, now, 1.0) * direction[p]
        yield

    def conclude(p):
        modeled = yield from model(p)
        curvature = 2.0 * total(jnp.sum(inverse[p] * modeled * modeled, axis=0, keepdims=True))
        yield
        spectra[p] += norms[p][0:1, 0:1] / jnp.where(curvature > 0.0, curvature, 1.0) * direction[p]
        yield

    def emit(chain, spread, order, hooks):
        pending = {p: chain(p) for p in order}
        key = {p: i * spread for i, p in enumerate(order)}
        while pending:
            p = min(pending, key=lambda q: (key[q], q))
            key[p] += count
            try:
                next(pending[p])
            except StopIteration:
                del pending[p]
            while hooks and not set(hooks[0][0]) & set(pending):
                hooks.pop(0)[1]()

    def whole_chain(p):
        yield from begin(p)
        for _ in range(ITERS - 1):
            yield from iterate(p)
        yield from conclude(p)

    pairs = count // 2
    per_half = pairs // 2
    marked = lane_index((32, LANES)) % (LANES // 2) == WPB
    blocks = [slice(0, LANES // 2), slice(LANES // 2, LANES)]
    cuts = [part.stop // FPB + 1 if part.stop < LANES else per_half for part in blocks]
    swaps = [
        pltpu.make_async_remote_copy(
            contrib.at[1 - core, part], arrived.at[part], swap_out.at[i], swap_in.at[i],
            device_id={"frame": partner}, device_id_type=MESH)
        for i, part in enumerate(blocks)
    ]

    def contribute(first, last, swap):
        for j in range(pairs):
            if not first <= j % per_half < last:
                continue
            scale = jnp.where(
                half,
                jnp.broadcast_to(weights[:, j:j + 1], (32, LANES)),
                jnp.broadcast_to(weights[:, pairs + j:pairs + j + 1], (32, LANES)))
            value = scale * jnp.where(marked, 1.0, jnp.where(half, spectra[j], spectra[pairs + j]))
            start = (j % per_half) * FPB
            contrib[j // per_half, start:start + FPB, :] = value[0:FPB]
        swap.start()

    for h in range(2):
        contrib[h, per_half * FPB:, :] = jnp.ones((LANES - per_half * FPB, LANES), f32)
    groups = [[p for p in every if p % per_half < cuts[0]], [p for p in every if p % per_half >= cuts[0]]]
    emit(whole_chain, SPREAD, groups[0] + groups[1], [
        (groups[0], lambda: contribute(0, cuts[0], swaps[0])),
        (groups[1], lambda: contribute(cuts[0], per_half, swaps[1])),
    ])
    spectra[count] = jnp.zeros((32, LANES), f32)

    for d in range(group):
        send[d] = jnp.where(half, spectra[source[d][0]], spectra[source[d][1]])[0:FPB]
    side = group // 2
    near = [lax.div(me, side) * side + lax.rem(me + k, side) for k in range(1, side)]
    far = [(1 - lax.div(me, side)) * side + lax.rem(me + k, side) for k in range(side)]
    spread = [
        pltpu.make_async_remote_copy(
            send.at[to], recv.at[me], out_sem.at[k], in_sem.at[k],
            device_id={"patch": to}, device_id_type=MESH)
        for k, to in enumerate(far + near)
    ]
    for copy in spread:
        copy.start()

    after, before = lax.rem(chip + 1, chips), lax.rem(chip + chips - 1, chips)

    def pass_on(owner, part, forward, out_sem, in_sem):
        return pltpu.make_async_remote_copy(
            gathered.at[owner, part], gathered.at[owner, part], out_sem, in_sem,
            device_id={"frame": 2 * (after if forward else before) + core}, device_id_type=MESH)

    for copy, part in zip(swaps, blocks):
        copy.wait_recv()
        gathered[chip, part, :] = contrib[core, part, :] + arrived[part, :]
    ahead = [pass_on(chip, part, True, direct_out.at[i], direct_in.at[i]) for i, part in enumerate(blocks)]
    back = [
        pass_on(chip, part, False, direct_out.at[2 + i], direct_in.at[2 + i])
        for i, part in enumerate(blocks)
    ]
    for copy in (ahead[0], back[1], ahead[1], back[0]):
        copy.start()
    recv[me] = send[me]
    ahead[0].wait_recv()
    relays = [pass_on(before, blocks[0], True, relay_out.at[0], relay_in.at[0])]
    relays[0].start()
    back[1].wait_recv()
    relays.append(pass_on(after, blocks[1], False, relay_out.at[1], relay_in.at[1]))
    relays[1].start()
    ahead[1].wait_recv()
    back[0].wait_recv()
    forward = []
    for i, part in enumerate(blocks):
        relays[i].wait_recv()
        whole = gathered[0, part, :]
        for k in range(1, chips):
            whole = whole + gathered[k, part, :]
        mass = jnp.where(
            lane_index(whole.shape) < LANES // 2,
            jnp.broadcast_to(whole[:, WPB:WPB + 1], whole.shape),
            jnp.broadcast_to(whole[:, LANES // 2 + WPB:LANES // 2 + WPB + 1], whole.shape))
        sums[core, part, :] = whole / mass
        forward.append(pltpu.make_async_remote_copy(
            sums.at[core, part], sums.at[core, part], fwd_out.at[i], fwd_in.at[i],
            device_id={"frame": partner}, device_id_type=MESH))
        forward[i].start()

    for copy in spread:
        copy.wait_recv()
    for k in range(FPB):
        rows = recv[:, k, :]
        ext_out[k, pl.ds(0, group, stride=2), :] = rows[:, 0:WPB]
        ext_out[k, pl.ds(1, group, stride=2), :] = pltpu.roll(rows, LANES // 2, 1)[:, 0:WPB]
    for copy in forward:
        copy.wait_recv()
    for k in range(FPB):
        for h in range(2):
            rows = sums[h, pl.ds(k, per_half, stride=FPB), :]
            for s in range(2):
                here = rows if s == 0 else pltpu.roll(rows, LANES // 2, 1)
                start = s * pairs + h * per_half
                coadd_out[k, start:start + per_half, :] = here[:, 0:WPB]
    down.wait_send()
    up.wait_send()
    for copy in swaps + ahead + back + relays + forward + spread:
        copy.wait_send()


def settle_kernel(ext_in, coadd_in, ext_out, coadd_out, sem):
    copies = [
        pltpu.make_async_copy(ext_in, ext_out, sem.at[0]),
        pltpu.make_async_copy(coadd_in, coadd_out, sem.at[1]),
    ]
    for copy in copies:
        copy.start()
    for copy in copies:
        copy.wait()


VMEM = pl.BlockSpec(memory_space=pltpu.VMEM)
SMEM = pl.BlockSpec(memory_space=pltpu.SMEM)
HBM = pl.BlockSpec(memory_space=pltpu.HBM)


def local(exposure, row_prof, col_prof, row_off, col_off, dest, fibre_weight):
    group = lax.axis_size("patch")
    frames = lax.axis_size("frame")
    count = dest.shape[1]
    chips = frames // 2
    f32, bf16 = jnp.float32, jnp.bfloat16
    _, channels, depth, width = exposure.shape
    tiles = width // LANES
    stride = -(-count // 8) * 8
    ext_out, coadd_out = pl.pallas_call(
        functools.partial(solve_kernel, count, group, frames),
        out_shape=(
            jax.ShapeDtypeStruct((FPB, 2 * group, WPB), f32),
            jax.ShapeDtypeStruct((FPB, count, WPB), f32),
        ),
        in_specs=[HBM] * 7,
        out_specs=(VMEM, VMEM),
        scratch_shapes=[
            pltpu.SMEM((1, count), jnp.int32),
            pltpu.SMEM((1, count), jnp.int32),
            pltpu.SMEM((1, count), jnp.int32),
            pltpu.VMEM((channels, depth, width), bf16),
            pltpu.VMEM((count, WPB, PR), bf16),
            pltpu.VMEM((FPB, count, PC), bf16),
            pltpu.VMEM((count, 1, FPB), f32),
            pltpu.VMEM((channels, HALO, width), bf16),
            pltpu.VMEM((channels, HALO, width), bf16),
            pltpu.VMEM((channels, tiles + 1, PR + HALO, LANES), f32),
            pltpu.VMEM((2, FPB * stride, LANES), f32),
            pltpu.VMEM((count, PR, LANES), bf16),
            pltpu.VMEM((count, 32, PC), bf16),
            pltpu.VMEM((count, 2, PR + HALO, LANES), f32),
            pltpu.VMEM((count, 2, PR + HALO, LANES), f32),
            pltpu.VMEM((count, PR, PC), f32),
            pltpu.VMEM((count, 32, LANES), f32),
            pltpu.VMEM((count, 32, LANES), f32),
            pltpu.VMEM((count + 1, 32, LANES), f32),
            pltpu.VMEM((count, 8, LANES), f32),
            pltpu.VMEM((group, FPB, LANES), f32),
            pltpu.VMEM((group, FPB, LANES), f32),
            pltpu.VMEM((2, LANES, LANES), f32),
            pltpu.VMEM((LANES, LANES), f32),
            pltpu.VMEM((chips, LANES, LANES), f32),
            pltpu.VMEM((2, LANES, LANES), f32),
            pltpu.SemaphoreType.DMA((7,)),
            pltpu.SemaphoreType.DMA((2,)),
            pltpu.SemaphoreType.DMA((2,)),
            pltpu.SemaphoreType.DMA((2,)),
            pltpu.SemaphoreType.DMA((2,)),
            pltpu.SemaphoreType.DMA((group,)),
            pltpu.SemaphoreType.DMA((group,)),
            pltpu.SemaphoreType.DMA((4,)),
            pltpu.SemaphoreType.DMA((4,)),
            pltpu.SemaphoreType.DMA((2,)),
            pltpu.SemaphoreType.DMA((2,)),
            pltpu.SemaphoreType.DMA((2,)),
            pltpu.SemaphoreType.DMA((2,)),
        ],
        compiler_params=pltpu.CompilerParams(
            collective_id=0, has_side_effects=True, vmem_limit_bytes=48 << 20),
        name="solve",
    )(
        *[pltpu.with_memory_space_constraint(a, pltpu.HBM) for a in (row_off, col_off, dest, exposure[0], row_prof[0],
        jnp.swapaxes(col_prof[0], 0, 1), jnp.swapaxes(fibre_weight, 0, 1))],
    )
    ext_out, coadd_out = pl.pallas_call(
        settle_kernel,
        out_shape=tuple(jax.ShapeDtypeStruct(a.shape, f32) for a in (ext_out, coadd_out)),
        in_specs=[VMEM] * 2,
        out_specs=(HBM, HBM),
        scratch_shapes=[pltpu.SemaphoreType.DMA((2,))],
        compiler_params=pltpu.CompilerParams(vmem_limit_bytes=8 << 20),
        name="settle",
    )(ext_out, coadd_out)
    return jnp.transpose(ext_out, (1, 2, 0))[None], jnp.transpose(coadd_out, (1, 2, 0))


def solution(mesh):
    in_specs = (
        P("frame", None, ("section", "patch"), None),
        P("frame", ("section", "patch"), None, None),
        P("frame", ("section", "patch"), None, None),
        P("frame", ("section", "patch")),
        P("frame", ("section", "patch")),
        P("frame", ("section", "patch")),
        P("frame", ("section", "patch"), None),
    )
    out_specs = (P("frame", ("section", "patch"), None, None), P(("section", "patch"), None, None))
    return jax.shard_map(local, mesh=mesh, in_specs=in_specs, out_specs=out_specs, check_vma=False)
```
